512 devices in a mesh: comp: 2 (over x_lo), tile: 128 (over z, x_hi, y), lev: 2 (over core).
Axes of the slice: x: 4 (x_hi: 2, x_lo: 2; x = x_hi * 2 + x_lo), y: 8, z: 8, core: 2. Of those that a mesh axis runs over, the one named last changes fastest.
Arguments:
- adj_final: float32 [2, 72, 32768], P('comp', 'lev', 'tile'), may hold values from -6 to 6
- flipped_vertical_steppers: float32 [2, 72, 72], P('comp', 'lev'), as said below
- profiles: float32 [2, 6, 72], P('comp', None, 'lev'), may hold values from -0.9 to 0.9
- skin_sensitivity_pair: float32 [2, 72], P('comp', 'lev'), may hold values from -0.9 to 0.9
- match: int32 [128], replicated, may hold values from 0 to 127, each once
- remap_offs: int32 [256, 4], P('tile'), may hold values from 0 to 5
- remap_count: int32 [256], P('tile'), may hold values from 1 to 4, as said below
- conserving_transfer_factors: float32 [256, 4, 128, 128], P('tile'), may hold values from -0.25 to 0.25
Outputs:
- adj_initial: float32 [2, 72, 32768], P('comp', 'lev', 'tile')
The draws below stay inside these ranges and needn't reach their ends.
Inputs may be any that keep to these rules, and one draw needn't show every extreme that they name: `match`: the atmosphere tiles in some order, each once. `remap_offs`: entries at or past a row block's count are to be ignored. `remap_count`: some row block uses all 4 entries. `flipped_vertical_steppers`: off-diagonal entries weigh about as much as the diagonal in each row.
All inputs are finite; a program needn't handle non-finite values.
Results may differ from the reference program's by a relative error of at most 0.00014.
Values sent between devices are 32-bit elements; how exact they have to be, the bound alone decides.
A program may use at most 64 MiB of HBM per device.

```python
import math
import jax
import jax.numpy as jnp
from jax import lax

LEVELS = 72
STEPS = 6
BLK = 128
NBMAX = 4
CELLS = 256
CELLS_ALL = 32768
TILE_BLOCKS = 2
BLOCKS = 256
N_TILE = 128


def draw_flipped_vertical_steppers(key, part):
    key_off, key_diag = jax.random.split(key)
    off_diagonal = jax.random.normal(key_off, (2, LEVELS, LEVELS), jnp.float32) * (0.15 / math.sqrt(LEVELS))
    diagonal = jax.random.uniform(key_diag, (2, LEVELS, 1), jnp.float32, 0.75, 1.0)
    diagonal_mask = jnp.eye(LEVELS, dtype=jnp.float32)[None]
    return off_diagonal * (1.0 - diagonal_mask) + diagonal * diagonal_mask


def draw_remap_count(key, part):
    key_tile, key_row = jax.random.split(key)
    tile_count = BLOCKS // TILE_BLOCKS
    busy_tile = jax.random.randint(key_tile, (tile_count,), 0, 4) == 3
    busy_row = jnp.repeat(busy_tile, TILE_BLOCKS, total_repeat_length=BLOCKS)
    reduction = jax.random.randint(key_row, (BLOCKS,), 0, 2)
    counts = jnp.where(busy_row, NBMAX - reduction, 1)
    counts = counts.at[0].set(NBMAX)
    return counts.astype(jnp.int32)


def set_ends(drawn, own_key, smallest, high):
    longest = drawn.shape.index(max(drawn.shape))
    spots = []
    for shift in (0, 1):
        where = [jax.random.randint(jax.random.fold_in(own_key, axis), (), 0, length) for axis, length in enumerate(drawn.shape)]
        where[longest] = (where[longest] + shift) % drawn.shape[longest]
        spots.append(tuple(where))
    return drawn.at[spots[0]].set(smallest).at[spots[1]].set(high)


def block_levels(rng, shape, shards, least, high):
    def one(dim, parts):
        draws = jax.random.uniform(jax.random.fold_in(jax.random.fold_in(rng, 6), dim), (parts,), jnp.float32, least / len(shards), high / len(shards))
        return jnp.repeat(jnp.exp(draws), shape[dim] // parts).reshape((-1,) + (1,) * (len(shape) - dim - 1))

    level = one(*shards[0])
    for cut in shards[1:]:
        level = level * one(*cut)
    return level


def normal_values(stream_key, dims, spread, bound, shards=(), kind=jnp.bfloat16):
    loudness = block_levels(stream_key, dims, shards, -0.22, 0.18) if shards else 1.0
    values = jax.random.normal(stream_key, dims, jnp.float32) * spread * loudness
    return jnp.minimum(jnp.maximum(values, -bound), bound).astype(kind)


def setup_inputs(seed: int = 0) -> dict:
    seeds = jax.random.split(jax.random.key(seed), 9)
    return {
        "adj_final": normal_values(seeds[0], (2, LEVELS, CELLS_ALL), 1.0, 6.0, ((0, 2), (1, 2), (2, 128)), jnp.float32),
        "flipped_vertical_steppers": draw_flipped_vertical_steppers(jax.random.fold_in(seeds[8], 71), 0),
        "profiles": normal_values(seeds[2], (2, STEPS, LEVELS), 0.15, 0.9, ((0, 2), (2, 2)), jnp.float32),
        "skin_sensitivity_pair": normal_values(seeds[3], (2, LEVELS), 0.15, 0.9, ((0, 2), (1, 2)), jnp.float32),
        "match": jax.random.permutation(seeds[4], N_TILE).astype(jnp.int32),
        "remap_offs": set_ends(jax.random.randint(seeds[5], (BLOCKS, NBMAX), 0, 3 * TILE_BLOCKS), jax.random.fold_in(seeds[5], 1), 0, (3 * TILE_BLOCKS) - 1).astype(jnp.int32),
        "remap_count": draw_remap_count(jax.random.fold_in(seeds[8], 71), 0),
        "conserving_transfer_factors": normal_values(seeds[7], (BLOCKS, NBMAX, BLK, BLK), (BLK * NBMAX) ** -0.5, 0.25, ((0, 128),), jnp.float32),
    }


HIGH_ACCURACY = lax.Precision.HIGHEST


def reference(adj_final, flipped_vertical_steppers, profiles, skin_sensitivity_pair, match, remap_offs, remap_count, conserving_transfer_factors):
    blocks = remap_offs.shape[0]
    tile_blocks = CELLS // BLK
    row_tile = jnp.arange(blocks, dtype=jnp.int32) // tile_blocks
    first_block = (match[row_tile] - 1) * tile_blocks
    target = jnp.mod(first_block[:, None] + remap_offs, blocks).astype(jnp.int32)
    in_use = (jnp.arange(NBMAX, dtype=jnp.int32)[None, :] < remap_count[:, None]).astype(jnp.float32)
    marine_backward_sensitivity = adj_final[1]
    phi_ocn = jnp.dot(profiles[1], marine_backward_sensitivity, precision=HIGH_ACCURACY)
    phi_rows = phi_ocn.reshape(STEPS, blocks, BLK).transpose(1, 0, 2)
    contrib = jnp.einsum("reij,rsi->resj", conserving_transfer_factors, phi_rows, precision=HIGH_ACCURACY) * in_use[:, :, None, None]
    phi_blocks = jnp.zeros((blocks, STEPS, BLK), jnp.float32).at[target.reshape(-1)].add(contrib.reshape(-1, STEPS, BLK))
    phi_atm = phi_blocks.transpose(1, 0, 2).reshape(STEPS, blocks * BLK)
    adjoint_atm = adj_final[0]
    surface_adj = jnp.zeros((blocks * BLK,), jnp.float32)
    for step in reversed(range(STEPS)):
        adjoint_atm = adjoint_atm + profiles[0, step][:, None] * phi_atm[step][None, :]
        surface_adj = surface_adj + jnp.dot(skin_sensitivity_pair[0], adjoint_atm, precision=HIGH_ACCURACY)
        adjoint_atm = jnp.dot(flipped_vertical_steppers[0], adjoint_atm, precision=HIGH_ACCURACY)
    chosen_tile_matrices = surface_adj.reshape(blocks, BLK)[target] * in_use[:, :, None]
    marine_skin_warmth = jnp.einsum("dcfv,dcv->df", conserving_transfer_factors, chosen_tile_matrices, precision=HIGH_ACCURACY).reshape(-1)
    marine_tile_matrix = jnp.dot(flipped_vertical_steppers[1], marine_backward_sensitivity, precision=HIGH_ACCURACY) + skin_sensitivity_pair[1][:, None] * marine_skin_warmth[None, :]
    return jnp.stack([adjoint_atm, marine_tile_matrix])
```

```python
import functools

import jax
import jax.numpy as jnp
from jax import lax
from jax.experimental import pallas as pl
from jax.experimental.pallas import tpu as pltpu
from jax.sharding import PartitionSpec as P

STEPS = 6
NBMAX = 4
HALF = STEPS // 2
F32 = jnp.float32
HIGHEST = lax.Precision.HIGHEST
MESH = pl.DeviceIdType.MESH


def dot(a, b):
    return jnp.dot(a, b, precision=HIGHEST, preferred_element_type=F32)


def column_of(row):
    n = row.shape[1]
    diagonal = lax.broadcasted_iota(jnp.int32, (n, n), 0) == lax.broadcasted_iota(
        jnp.int32, (n, n), 1
    )
    return jnp.sum(jnp.where(diagonal, row, 0.0), axis=1, keepdims=True)


def kernel(
    nz,
    nw,
    match_ref,
    offs_ref,
    count_ref,
    adj_ref,
    operator_ref,
    profile_ref,
    skin_ref,
    factors_hbm,
    out_ref,
    factors,
    state,
    operators,
    profiles,
    skins,
    flux_part,
    flux_half,
    contrib_in,
    row_out,
    row_in,
    sigma_own,
    sigma_row,
    pick_out,
    pick_in,
    powers,
    local_sem,
    pair_send,
    pair_recv,
    flux_send,
    flux_recv,
    contrib_send,
    contrib_recv,
    row_send,
    row_recv,
    sigma_send,
    sigma_recv,
    pick_send,
    pick_recv,
):
    comp = lax.axis_index("comp")
    lev = lax.axis_index("lev")
    tile = lax.axis_index("tile")
    tiles = nz * nw
    z = tile // nw
    w = tile % nw
    levels = adj_ref.shape[1]
    blk = factors.shape[2]
    rows = factors.shape[0]

    def remote(src, dst, send, recv, to_comp, to_tile, to_lev):
        copy = pltpu.make_async_remote_copy(
            src_ref=src,
            dst_ref=dst,
            send_sem=send,
            recv_sem=recv,
            device_id=(to_comp, to_tile, to_lev),
            device_id_type=MESH,
        )
        copy.start()

    def settle(ref, sem):
        pltpu.make_async_copy(ref, ref, sem).wait()

    load = pltpu.make_async_copy(factors_hbm, factors, local_sem)
    load.start()

    own = adj_ref[0]
    state[lev] = own

    @pl.when(comp == 1)
    def _():
        partial = dot(profile_ref[0], own)
        flux_part[0] = partial[:HALF]
        flux_part[1] = partial[HALF:]
        remote(flux_part.at[1 - lev], flux_half.at[lev], flux_send, flux_recv, 1, tile, 1 - lev)
        for half in range(2):
            remote(flux_part.at[half], flux_half.at[lev], flux_send, flux_recv, 0, tile, half)
        flux_half[lev] = flux_part[lev]

    operators[lev] = operator_ref[0]
    profiles[lev] = profile_ref[0]
    skins[lev] = skin_ref[...]
    for ref, i in ((state, 0), (operators, 1), (profiles, 2), (skins, 3)):
        remote(ref.at[lev], ref.at[lev], pair_send.at[i], pair_recv.at[i], comp, tile, 1 - lev)

    load.wait()

    @pl.when(comp == 1)
    def _():
        settle(flux_half.at[0], flux_recv)

    @pl.when(comp == 0)
    def _():
        settle(flux_half, flux_recv)

    flux = flux_half[0] + flux_half[1]
    flux = jnp.concatenate([flux, jnp.zeros((8 - HALF, flux.shape[1]), F32)], axis=0).T
    totals = [jnp.zeros((HALF, blk), F32) for _ in range(3)]
    for r in range(rows):
        columns = [
            jnp.broadcast_to(flux[r * blk : (r + 1) * blk, s : s + 1], (blk, blk))
            for s in range(HALF)
        ]
        for e in range(NBMAX):
            block = factors[r, e]
            part = jnp.concatenate(
                [jnp.sum(block * columns[s], axis=0, keepdims=True) for s in range(HALF)], axis=0
            )
            offset = offs_ref[r, e]
            used = e < count_ref[r]
            for d in range(3):
                take = jnp.logical_and(used, offset == 2 * d + comp)
                totals[d] = totals[d] + part * take.astype(F32)
    for d in range(3):
        contrib_in[z, d] = totals[d]
    for k in range(1, nz):
        to = (z + k) % nz
        remote(
            contrib_in.at[z], contrib_in.at[z], contrib_send, contrib_recv, comp, to * nw + w, lev
        )

    held = [match_ref[i * nw + w] for i in range(nz)]
    origin, present = [], []
    for p in range(nw + 2):
        wanted = (z * nw - 1 + p + tiles) % tiles
        found = jnp.int32(-1)
        for i in range(nz):
            found = jnp.where(held[i] == wanted, i, found)
        origin.append(jnp.maximum(found, 0))
        present.append((found >= 0).astype(F32))

    for i, ref in enumerate((state, operators, profiles, skins)):
        settle(ref.at[0], pair_recv.at[i])
    whole = jnp.concatenate([operators[0], operators[1]], axis=0)
    skin_row = jnp.concatenate([skins[0], skins[1]], axis=1)
    profile_rows = jnp.concatenate([profiles[0], profiles[1]], axis=1)
    powers[0, :levels] = operator_ref[0]
    powers[0, levels : levels + 1] = skin_row

    @pl.when(comp == 0)
    def _():
        held_power = powers[0, : levels + 1]
        last = held_power[levels:]
        for n in range(1, STEPS):
            held_power = dot(held_power, whole)
            last = last + held_power[levels:]
            powers[n, :levels] = held_power[:levels]
            powers[n, levels : levels + 1] = last

    settle(contrib_in.at[: nz - 1], contrib_recv)

    for q in range(nw):
        total = jnp.zeros((HALF, blk), F32)
        for d in range(3):
            p = q + 2 - d
            total = total + contrib_in[origin[p], d] * present[p]
        row_out[q] = total
    slot = (comp * 2 + lev) * nw + w
    for k in range(nw):
        to = (w + k) % nw
        for half in range(2):
            if k == 0:
                here = jnp.logical_and(comp == 0, lev == half)

                @pl.when(here)
                def _():
                    row_in[slot] = row_out[w]

                @pl.when(jnp.logical_not(here))
                def _():
                    remote(
                        row_out.at[to], row_in.at[slot], row_send, row_recv, 0, z * nw + to, half
                    )

            else:
                remote(row_out.at[to], row_in.at[slot], row_send, row_recv, 0, z * nw + to, half)

    full_state = jnp.concatenate([state[0], state[1]], axis=0)

    @pl.when(comp == 0)
    def _():
        base = dot(powers[STEPS - 1, : levels + 1], full_state)
        shares = [
            jnp.sum(powers[s, : levels + 1] * profile_rows[s : s + 1], axis=1, keepdims=True)
            for s in range(STEPS)
        ]
        settle(row_in.at[: 4 * nw - 1], row_recv)
        halves = []
        for parity in range(2):
            cells = slice(parity * blk, (parity + 1) * blk)
            total = base[:, cells]
            for half in range(2):
                start = (parity * 2 + half) * nw
                flux_sum = row_in[start]
                for k in range(1, nw):
                    flux_sum = flux_sum + row_in[start + k]
                for s in range(HALF):
                    total = total + shares[half * HALF + s] * flux_sum[s : s + 1]
            sigma_own[parity : parity + 1] = total[levels:]
            halves.append(total)
        for k in range(nw):
            to = (w + k) % nw
            remote(sigma_own, sigma_row.at[w], sigma_send, sigma_recv, 1, z * nw + to, lev)
        for parity in range(2):
            out_ref[0, :, parity * blk : (parity + 1) * blk] = halves[parity][:levels]

    @pl.when(comp == 1)
    def _():
        base = dot(powers[0, :levels], full_state)
        settle(sigma_row, sigma_recv)
        for i in range(nz):
            first = match_ref[i * nw + w] - 1 + tiles
            for d in range(3):
                pick_out[i, d] = sigma_row[(first + d) % nw]
        for k in range(1, nz):
            to = (z + k) % nz
            remote(pick_out.at[to], pick_in.at[z], pick_send, pick_recv, 1, to * nw + w, lev)
        pick_in[z] = pick_out[z]
        settle(pick_in.at[: nz - 1], pick_recv)
        first = match_ref[tile] - 1 + tiles
        home = [((first + d) % tiles) // nw for d in range(3)]
        skin_column = jnp.broadcast_to(column_of(skin_ref[...]), (levels, blk))
        for r in range(rows):
            total = jnp.zeros((blk, blk), F32)
            for e in range(NBMAX):
                offset = offs_ref[r, e]
                used = (e < count_ref[r]).astype(F32)
                third = offset // 2
                where = jnp.where(third == 0, home[0], jnp.where(third == 1, home[1], home[2]))
                sigma = pick_in[where, third, pl.ds(offset % 2, 1)] * used
                total = total + factors[r, e] * sigma
            warmth = lax.dot_general(
                skin_column,
                total,
                (((1,), (1,)), ((), ())),
                precision=HIGHEST,
                preferred_element_type=F32,
            )
            cells = slice(r * blk, (r + 1) * blk)
            out_ref[0, :, cells] = base[:, cells] + warmth

    for i, ref in enumerate((state, operators, profiles, skins)):
        settle(ref.at[0], pair_send.at[i])
    settle(contrib_in.at[: nz - 1], contrib_send)

    @pl.when(comp == 0)
    def _():
        settle(row_in.at[: 2 * nw - 1], row_send)
        settle(sigma_row, sigma_send)

    @pl.when(comp == 1)
    def _():
        settle(row_in.at[: 2 * nw], row_send)
        settle(flux_part, flux_send)
        settle(pick_in.at[: nz - 1], pick_send)


def on_device(
    adj_final,
    flipped_vertical_steppers,
    profiles,
    skin_sensitivity_pair,
    match,
    remap_offs,
    remap_count,
    conserving_transfer_factors,
):
    tiles = lax.axis_size("tile")
    nz = 2 ** ((tiles.bit_length() - 1) // 2)
    nw = tiles // nz
    levels, cells = adj_final.shape[1:]
    rows, _, blk, _ = conserving_transfer_factors.shape
    vmem = pl.BlockSpec(memory_space=pltpu.VMEM)
    smem = pl.BlockSpec(memory_space=pltpu.SMEM)
    dma = pltpu.SemaphoreType.DMA
    return pl.pallas_call(
        functools.partial(kernel, nz, nw),
        out_shape=jax.ShapeDtypeStruct(adj_final.shape, F32),
        in_specs=[smem] * 3 + [vmem] * 4 + [pl.BlockSpec(memory_space=pl.ANY)],
        out_specs=vmem,
        scratch_shapes=[
            pltpu.VMEM((rows, NBMAX, blk, blk), F32),
            pltpu.VMEM((2, levels, cells), F32),
            pltpu.VMEM((2, levels, 2 * levels), F32),
            pltpu.VMEM((2, STEPS, levels), F32),
            pltpu.VMEM((2, 1, levels), F32),
            pltpu.VMEM((3, HALF, cells), F32),
            pltpu.VMEM((2, HALF, cells), F32),
            pltpu.VMEM((nz, 3, HALF, blk), F32),
            pltpu.VMEM((nw, HALF, blk), F32),
            pltpu.VMEM((4 * nw, HALF, blk), F32),
            pltpu.VMEM((2, blk), F32),
            pltpu.VMEM((nw, 2, blk), F32),
            pltpu.VMEM((nz, 3, 2, blk), F32),
            pltpu.VMEM((nz, 3, 2, blk), F32),
            pltpu.VMEM((STEPS, levels + 4, 2 * levels), F32),
            dma,
            dma((4,)),
            dma((4,)),
        ]
        + [dma] * 10,
        compiler_params=pltpu.CompilerParams(has_side_effects=True, vmem_limit_bytes=32 << 20),
    )(
        match,
        remap_offs,
        remap_count,
        adj_final,
        flipped_vertical_steppers,
        profiles,
        skin_sensitivity_pair,
        conserving_transfer_factors,
    )


def solution(mesh):
    return jax.shard_map(
        on_device,
        mesh=mesh,
        in_specs=(
            P("comp", "lev", "tile"),
            P("comp", "lev", None),
            P("comp", None, "lev"),
            P("comp", "lev"),
            P(),
            P("tile", None),
            P("tile"),
            P("tile", None, None, None),
        ),
        out_specs=P("comp", "lev", "tile"),
        check_vma=False,
    )
```

```python
import functools

import jax
import jax.numpy as jnp
from jax import lax
from jax.experimental import pallas as pl
from jax.experimental.pallas import tpu as pltpu
from jax.sharding import PartitionSpec as P

STEPS = 6
NBMAX = 4
HALF = STEPS // 2
F32 = jnp.float32
HIGHEST = lax.Precision.HIGHEST
MESH = pl.DeviceIdType.MESH
REACH = 6
GROUP = 8


def dot(a, b):
    return jnp.dot(a, b, precision=HIGHEST, preferred_element_type=F32)


def column_of(row):
    n = row.shape[1]
    diagonal = lax.broadcasted_iota(jnp.int32, (n, n), 0) == lax.broadcasted_iota(
        jnp.int32, (n, n), 1
    )
    return jnp.sum(jnp.where(diagonal, row, 0.0), axis=1, keepdims=True)


def kernel(
    nz,
    nw,
    match_hbm,
    offs_hbm,
    count_hbm,
    adj_hbm,
    operator_hbm,
    profile_hbm,
    skin_hbm,
    factors_hbm,
    out_ref,
    match_ref,
    offs_ref,
    count_ref,
    factors,
    state,
    operators,
    profiles,
    skins,
    flux_part,
    flux_half,
    contrib_in,
    weight_in,
    sigma_own,
    sigma_in,
    mixed,
    flux_out,
    flux_in,
    flux_sum,
    heat_out,
    heat_in,
    heat_sum,
    heat,
    load_sem,
    pair_send,
    pair_recv,
    part_send,
    part_recv,
    contrib_send,
    contrib_recv,
    weight_send,
    weight_recv,
    sigma_send,
    sigma_recv,
    flux_send,
    flux_recv,
    heat_send,
    heat_recv,
    last_send,
    last_recv,
):
    comp = lax.axis_index("comp")
    lev = lax.axis_index("lev")
    tile = lax.axis_index("tile")
    tiles = nz * nw
    z = tile // nw
    w = tile % nw
    levels = operators.shape[1]
    blk = factors.shape[2]
    rows = factors.shape[0]
    column = [((z + k) % nz) * nw + w for k in range(nz)]
    row = [z * nw + (w + k) % nw for k in range(nw)]
    atmos, ocean = comp == 0, comp == 1

    def remote(src, dst, send, recv, to_comp, to_tile, to_lev):
        pltpu.make_async_remote_copy(
            src_ref=src,
            dst_ref=dst,
            send_sem=send,
            recv_sem=recv,
            device_id=(to_comp, to_tile, to_lev),
            device_id_type=MESH,
        ).start()

    def settle(ref, sem):
        pltpu.make_async_copy(ref, ref, sem).wait()

    def halves(ref):
        return [ref[pl.ds(h, levels, stride=2), :] for h in range(2)]

    loads = [
        pltpu.make_async_copy(src, dst, load_sem.at[i])
        for i, (src, dst) in enumerate(
            (
                (adj_hbm, state.at[lev]),
                (profile_hbm.at[0], profiles.at[lev]),
                (operator_hbm.at[0], operators.at[lev]),
                (skin_hbm, skins.at[lev]),
                (factors_hbm, factors),
                (offs_hbm, offs_ref),
                (count_hbm, count_ref),
                (match_hbm, match_ref),
            )
        )
    ]
    for load in loads:
        load.start()

    barrier = pltpu.get_barrier_semaphore()

    def greet(to_comp, to_tile, to_lev):
        pl.semaphore_signal(
            barrier, inc=1, device_id=(to_comp, to_tile, to_lev), device_id_type=MESH
        )

    greet(comp, tile, 1 - lev)

    @pl.when(atmos)
    def _():
        for to in row:
            greet(1, to, lev)
        pl.semaphore_wait(barrier, 1 + nz)

    @pl.when(ocean)
    def _():
        for to in column:
            greet(0, to, lev)
        for to in column[1:] + row[1:]:
            greet(1, to, lev)
        pl.semaphore_wait(barrier, nz + 2 * nw - 1)

    pairs = (
        (adj_hbm, state),
        (operator_hbm.at[0], operators),
        (profile_hbm.at[0], profiles),
        (skin_hbm, skins),
    )

    @pl.when(atmos)
    def _():
        for i, (src, dst) in ((1, pairs[1]), (3, pairs[3]), (2, pairs[2]), (0, pairs[0])):
            remote(src, dst.at[lev], pair_send.at[i], pair_recv.at[i], 0, tile, 1 - lev)
        for load in loads[:4]:
            load.wait()
        for i in (1, 2, 3):
            settle(pairs[i][1].at[0], pair_recv.at[i])
        whole = jnp.concatenate([operators[0], operators[1]], axis=0)
        profile_rows = jnp.concatenate([profiles[0], profiles[1]], axis=1)

        power = jnp.concatenate([skins[0], skins[1]], axis=1)
        total = power
        for s in range(STEPS):
            if s > 0:
                power = dot(power, whole)
                total = total + power
            weight = jnp.sum(total * profile_rows[s : s + 1], axis=1, keepdims=True)
            weight_in[1, s : s + 1] = jnp.broadcast_to(weight, (1, blk))
        remote(weight_in.at[1], weight_in.at[0], weight_send, weight_recv, 1, tile, lev)
        mine = jnp.where(lev == 0, total[:, :levels], total[:, levels:])
        own = halves(state.at[lev])
        for h in range(2):
            sigma_own[h : h + 1] = dot(mine, own[h])
        for to in column:
            remote(sigma_own, sigma_in.at[z], sigma_send, sigma_recv, 1, to, lev)

        power = operators[lev]
        shares = []
        for s in range(STEPS):
            if s > 0:
                power = dot(power, whole)
            shares.append(jnp.sum(power * profile_rows[s : s + 1], axis=1, keepdims=True))
        settle(state.at[0], pair_recv.at[0])
        first, second = halves(state.at[0]), halves(state.at[1])
        bases = [dot(power, jnp.concatenate([first[h], second[h]], axis=0)) for h in range(2)]

        settle(flux_in, flux_recv)
        total = flux_in[0]
        for k in range(1, nw):
            total = total + flux_in[k]
        flux_sum[lev] = total
        remote(flux_sum.at[lev], flux_sum.at[lev], last_send, last_recv, 0, tile, 1 - lev)
        settle(flux_sum.at[0], last_recv)
        for h in range(2):
            total = bases[h]
            for s in range(STEPS):
                total = total + shares[s] * flux_sum[s // HALF, s % HALF, h : h + 1]
            out_ref[pl.ds(h, levels, stride=2), :] = total

        for i in range(4):
            settle(pairs[i][1].at[0], pair_send.at[i])
        settle(weight_in.at[0], weight_send)
        settle(sigma_in, sigma_send)
        settle(flux_sum.at[0], last_send)
        for load in loads[4:]:
            load.wait()

    @pl.when(ocean)
    def _():
        for load in loads[:2]:
            load.wait()
        own = halves(state.at[lev])
        for h in range(2):
            partial = dot(profiles[lev], own[h])
            for half in range(2):
                flux_part[half, h] = partial[half * HALF : (half + 1) * HALF]
        remote(
            flux_part.at[1 - lev], flux_half.at[lev], part_send, part_recv, 1, tile, 1 - lev
        )
        remote(adj_hbm, state.at[lev], pair_send.at[0], pair_recv.at[0], 1, tile, 1 - lev)
        flux_half[lev] = flux_part[lev]
        contrib_in[:, :, REACH:] = jnp.zeros((nz, HALF, GROUP - REACH, blk), F32)
        for load in loads[4:]:
            load.wait()
        settle(flux_half.at[0], part_recv)

        totals = [jnp.zeros((HALF, blk), F32) for _ in range(REACH)]
        for r in range(rows):
            flux = flux_half[0, r] + flux_half[1, r]
            flux = jnp.concatenate([flux, jnp.zeros((GROUP - HALF, blk), F32)], axis=0).T
            columns = [jnp.broadcast_to(flux[:, s : s + 1], (blk, blk)) for s in range(HALF)]
            for e in range(NBMAX):
                block = factors[r, e]
                part = jnp.concatenate(
                    [jnp.sum(block * columns[s], axis=0, keepdims=True) for s in range(HALF)],
                    axis=0,
                )
                offset = jnp.where(e < count_ref[r], offs_ref[r, e], -1)
                for b in range(REACH):
                    totals[b] = totals[b] + part * (offset == b).astype(F32)
        for s in range(HALF):
            contrib_in[z, s, :REACH] = jnp.concatenate(
                [totals[b][s : s + 1] for b in range(REACH)], axis=0
            )
        for to in column[1:]:
            remote(
                contrib_in.at[z, :, pl.ds(0, REACH)],
                contrib_in.at[z, :, pl.ds(0, REACH)],
                contrib_send,
                contrib_recv,
                1,
                to,
                lev,
            )

        size = nz * GROUP
        lane = lax.broadcasted_iota(jnp.int32, (GROUP, size), 1)
        sub = lax.broadcasted_iota(jnp.int32, (GROUP, size), 0)
        place, source = lane % GROUP, lane // GROUP
        have = jnp.zeros((GROUP, size), jnp.int32)
        for i in range(nz):
            have = jnp.where(source == i, match_ref[i * nw + w] - 1, have)
        have = jnp.where(place < REACH, have + place // 2, source * nw + w)
        same = (lane % 2) == (sub % 2)
        picks = []
        for q in range(0, nw, 4):
            wanted = z * nw + q + sub // 2
            hit = jnp.bitwise_and(have - wanted, tiles - 1) == 0
            hit = jnp.logical_and(jnp.logical_and(hit, same), place < REACH)
            picks.append(hit.astype(F32))
        to_atmos = jnp.concatenate(picks, axis=0)[: 2 * nw]
        picks = []
        for q in range(nw):
            wanted = match_ref[z * nw + q] - 1 + sub // 2
            hit = jnp.bitwise_and(have - wanted, tiles - 1) == 0
            hit = jnp.logical_and(jnp.logical_and(hit, same), sub < REACH)
            picks.append(hit.astype(F32))
        to_ocean = jnp.concatenate(picks, axis=0)

        for load in loads[2:4]:
            load.wait()
        settle(state.at[0], pair_recv.at[0])
        first, second = halves(state.at[0]), halves(state.at[1])
        bases = [
            dot(operators[lev], jnp.concatenate([first[h], second[h]], axis=0)) for h in range(2)
        ]
        skin_column = jnp.broadcast_to(column_of(skins[lev]), (levels, blk))

        settle(contrib_in.at[: nz - 1, :, pl.ds(0, REACH)], contrib_recv)
        column_data = [contrib_in[:, s].reshape(size, blk) for s in range(HALF)]
        for s in range(HALF):
            picked = dot(to_atmos, column_data[s])
            for q in range(nw):
                flux_out[q, s] = picked[2 * q : 2 * q + 2]
        for k in range(nw):
            remote(
                flux_out.at[(w + k) % nw], flux_in.at[w], flux_send, flux_recv, 0, row[k], lev
            )
        settle(weight_in.at[0], weight_recv)
        total = jnp.zeros((size, blk), F32)
        for s in range(HALF):
            weight = jnp.where(
                lev == 0, weight_in[0, s : s + 1], weight_in[0, HALF + s : HALF + s + 1]
            )
            total = total + weight * column_data[s]
        mixed[...] = total
        settle(sigma_in, sigma_recv)
        for i in range(nz):
            mixed[i * GROUP + REACH : (i + 1) * GROUP] = sigma_in[i]
        heat_out[...] = dot(to_ocean, mixed[...]).reshape(nw, GROUP, blk)
        for k in range(1, nw):
            remote(
                heat_out.at[(w + k) % nw], heat_in.at[w], heat_send, heat_recv, 1, row[k], lev
            )
        heat_in[w] = heat_out[w]
        settle(heat_in.at[: nw - 1], heat_recv)
        total = heat_in[0]
        for k in range(1, nw):
            total = total + heat_in[k]
        heat_sum[lev] = total
        remote(heat_sum.at[lev], heat_sum.at[lev], last_send, last_recv, 1, tile, 1 - lev)
        settle(heat_sum.at[0], last_recv)
        heat[...] = heat_sum[0] + heat_sum[1]
        for r in range(rows):
            total = jnp.zeros((blk, blk), F32)
            for e in range(NBMAX):
                used = (e < count_ref[r]).astype(F32)
                total = total + factors[r, e] * (heat[pl.ds(offs_ref[r, e], 1), :] * used)
            warmth = lax.dot_general(
                skin_column,
                total,
                (((1,), (1,)), ((), ())),
                precision=HIGHEST,
                preferred_element_type=F32,
            )
            out_ref[pl.ds(r, levels, stride=2), :] = bases[r] + warmth

        settle(flux_part.at[0], part_send)
        settle(state.at[0], pair_send.at[0])
        settle(contrib_in.at[: nz - 1, :, pl.ds(0, REACH)], contrib_send)
        settle(flux_in, flux_send)
        settle(heat_in.at[: nw - 1], heat_send)
        settle(heat_sum.at[0], last_send)


def on_device(
    adj_final,
    flipped_vertical_steppers,
    profiles,
    skin_sensitivity_pair,
    match,
    remap_offs,
    remap_count,
    conserving_transfer_factors,
):
    tiles = lax.axis_size("tile")
    nz = 2 ** ((tiles.bit_length() - 1) // 2)
    nw = tiles // nz
    levels, cells = adj_final.shape[1:]
    rows, _, blk, _ = conserving_transfer_factors.shape
    hbm = pl.BlockSpec(memory_space=pltpu.HBM)
    dma = pltpu.SemaphoreType.DMA
    out = pl.pallas_call(
        functools.partial(kernel, nz, nw),
        out_shape=jax.ShapeDtypeStruct((levels * rows, blk), F32),
        in_specs=[hbm] * 8,
        out_specs=pl.BlockSpec(memory_space=pltpu.VMEM),
        scratch_shapes=[
            pltpu.SMEM(match.shape, jnp.int32),
            pltpu.SMEM(remap_offs.shape, jnp.int32),
            pltpu.SMEM(remap_count.shape, jnp.int32),
            pltpu.VMEM((rows, NBMAX, blk, blk), F32),
            pltpu.VMEM((2, levels * rows, blk), F32),
            pltpu.VMEM((2, levels, 2 * levels), F32),
            pltpu.VMEM((2, STEPS, levels), F32),
            pltpu.VMEM((2, 1, levels), F32),
            pltpu.VMEM((2, 2, HALF, blk), F32),
            pltpu.VMEM((2, 2, HALF, blk), F32),
            pltpu.VMEM((nz, HALF, GROUP, blk), F32),
            pltpu.VMEM((2, GROUP, blk), F32),
            pltpu.VMEM((2, blk), F32),
            pltpu.VMEM((nz, 2, blk), F32),
            pltpu.VMEM((nz * GROUP, blk), F32),
            pltpu.VMEM((nw, HALF, 2, blk), F32),
            pltpu.VMEM((nw, HALF, 2, blk), F32),
            pltpu.VMEM((2, HALF, 2, blk), F32),
            pltpu.VMEM((nw, GROUP, blk), F32),
            pltpu.VMEM((nw, GROUP, blk), F32),
            pltpu.VMEM((2, GROUP, blk), F32),
            pltpu.VMEM((GROUP, blk), F32),
            dma((8,)),
            dma((4,)),
            dma((4,)),
        ]
        + [dma] * 14,
        compiler_params=pltpu.CompilerParams(
            has_side_effects=True, collective_id=0, vmem_limit_bytes=32 << 20
        ),
    )(
        match,
        remap_offs,
        remap_count,
        adj_final.reshape(levels * rows, blk),
        flipped_vertical_steppers,
        profiles,
        skin_sensitivity_pair,
        conserving_transfer_factors,
    )
    return out.reshape(1, levels, cells)


def solution(mesh):
    return jax.shard_map(
        on_device,
        mesh=mesh,
        in_specs=(
            P("comp", "lev", "tile"),
            P("comp", "lev", None),
            P("comp", None, "lev"),
            P("comp", "lev"),
            P(),
            P("tile", None),
            P("tile"),
            P("tile", None, None, None),
        ),
        out_specs=P("comp", "lev", "tile"),
        check_vma=False,
    )
```

```python
import functools

import jax
import jax.numpy as jnp
from jax import lax
from jax.experimental import pallas as pl
from jax.experimental.pallas import tpu as pltpu
from jax.sharding import PartitionSpec as P

STEPS = 6
NBMAX = 4
HALF = STEPS // 2
F32 = jnp.float32
HIGHEST = lax.Precision.HIGHEST
MESH = pl.DeviceIdType.MESH
REACH = 6
GROUP = 8


def dot(a, b):
    return jnp.dot(a, b, precision=HIGHEST, preferred_element_type=F32)


def column_of(row):
    n = row.shape[1]
    diagonal = lax.broadcasted_iota(jnp.int32, (n, n), 0) == lax.broadcasted_iota(
        jnp.int32, (n, n), 1
    )
    return jnp.sum(jnp.where(diagonal, row, 0.0), axis=1, keepdims=True)


def kernel(
    nz,
    nw,
    match_hbm,
    offs_hbm,
    count_hbm,
    adj_hbm,
    operator_hbm,
    profile_hbm,
    skin_hbm,
    factors_hbm,
    out_ref,
    match_ref,
    offs_ref,
    count_ref,
    factors,
    state,
    operators,
    profiles,
    skins,
    flux_part,
    flux_half,
    contrib_in,
    weight_in,
    sigma_own,
    sigma_in,
    mixed,
    flux_out,
    flux_in,
    flux_sum,
    heat_out,
    heat_in,
    heat_sum,
    heat,
    load_sem,
    pair_send,
    pair_recv,
    part_send,
    part_recv,
    contrib_send,
    contrib_recv,
    weight_send,
    weight_recv,
    sigma_send,
    sigma_recv,
    flux_send,
    flux_recv,
    heat_send,
    heat_recv,
    last_send,
    last_recv,
):
    comp = lax.axis_index("comp")
    lev = lax.axis_index("lev")
    tile = lax.axis_index("tile")
    tiles = nz * nw
    z = tile // nw
    w = tile % nw
    levels = operators.shape[1]
    blk = factors.shape[2]
    rows = factors.shape[0]
    ny = nw // 2
    far = sorted(range(nz), key=lambda k: -min(k, nz - k))
    column = [((z + k) % nz) * nw + w for k in far]
    far = sorted(
        ((i, k) for i in range(2) for k in range(ny)),
        key=lambda ik: -(2 * ik[0] + min(ik[1], ny - ik[1])),
    )
    steps = [((w // ny + i) % 2) * ny + (w % ny + k) % ny for i, k in far]
    row = [z * nw + q for q in steps]
    atmos, ocean = comp == 0, comp == 1

    def remote(src, dst, send, recv, to_comp, to_tile, to_lev):
        pltpu.make_async_remote_copy(
            src_ref=src,
            dst_ref=dst,
            send_sem=send,
            recv_sem=recv,
            device_id=(to_comp, to_tile, to_lev),
            device_id_type=MESH,
        ).start()

    def settle(ref, sem):
        pltpu.make_async_copy(ref, ref, sem).wait()

    def halves(ref):
        return [ref[pl.ds(h, levels, stride=2), :] for h in range(2)]

    loads = [
        pltpu.make_async_copy(src, dst, load_sem.at[i])
        for i, (src, dst) in enumerate(
            (
                (adj_hbm, state.at[lev]),
                (profile_hbm, profiles.at[lev]),
                (operator_hbm, operators.at[lev]),
                (skin_hbm, skins.at[lev]),
                (factors_hbm, factors),
                (offs_hbm, offs_ref),
                (count_hbm, count_ref),
                (match_hbm, match_ref),
            )
        )
    ]
    for load in loads:
        load.start()

    barrier = pltpu.get_barrier_semaphore()

    def greet(to_comp, to_tile, to_lev):
        pl.semaphore_signal(
            barrier, inc=1, device_id=(to_comp, to_tile, to_lev), device_id_type=MESH
        )

    greet(comp, tile, 1 - lev)

    @pl.when(atmos)
    def _():
        for to in row:
            greet(1, to, lev)
        pl.semaphore_wait(barrier, 1 + nz)

    @pl.when(ocean)
    def _():
        for to in column:
            greet(0, to, lev)
        for to in column[:-1] + row[:-1]:
            greet(1, to, lev)
        pl.semaphore_wait(barrier, nz + 2 * nw - 1)

    pairs = (
        (adj_hbm, state),
        (operator_hbm, operators),
        (profile_hbm, profiles),
        (skin_hbm, skins),
    )

    @pl.when(atmos)
    def _():
        for i, (src, dst) in ((1, pairs[1]), (3, pairs[3]), (2, pairs[2]), (0, pairs[0])):
            remote(src, dst.at[lev], pair_send.at[i], pair_recv.at[i], 0, tile, 1 - lev)
        for load in loads[:4]:
            load.wait()
        for i in (1, 2, 3):
            settle(pairs[i][1].at[0], pair_recv.at[i])
        whole = jnp.concatenate([operators[0, :, 0], operators[1, :, 0]], axis=0)
        profile_rows = jnp.concatenate([profiles[0, :, 0], profiles[1, :, 0]], axis=1)

        power = jnp.concatenate([skins[0], skins[1]], axis=1)
        total = power
        for s in range(STEPS):
            if s > 0:
                power = dot(power, whole)
                total = total + power
            weight = jnp.sum(total * profile_rows[s : s + 1], axis=1, keepdims=True)
            weight_in[1, s : s + 1] = jnp.broadcast_to(weight, (1, blk))
        remote(weight_in.at[1], weight_in.at[0], weight_send, weight_recv, 1, tile, lev)
        mine = jnp.where(lev == 0, total[:, :levels], total[:, levels:])
        own = halves(state.at[lev])
        for h in range(2):
            sigma_own[h : h + 1] = dot(mine, own[h])
        for to in column:
            remote(sigma_own, sigma_in.at[z], sigma_send, sigma_recv, 1, to, lev)

        power = operators[lev, :, 0]
        shares = []
        for s in range(STEPS):
            if s > 0:
                power = dot(power, whole)
            shares.append(jnp.sum(power * profile_rows[s : s + 1], axis=1, keepdims=True))
        settle(state.at[0], pair_recv.at[0])
        first, second = halves(state.at[0]), halves(state.at[1])
        bases = [dot(power, jnp.concatenate([first[h], second[h]], axis=0)) for h in range(2)]

        settle(flux_in, flux_recv)
        total = flux_in[0]
        for k in range(1, nw):
            total = total + flux_in[k]
        flux_sum[lev] = total
        remote(flux_sum.at[lev], flux_sum.at[lev], last_send, last_recv, 0, tile, 1 - lev)
        settle(flux_sum.at[0], last_recv)
        for h in range(2):
            total = bases[h]
            for s in range(STEPS):
                total = total + shares[s] * flux_sum[s // HALF, s % HALF, h : h + 1]
            out_ref[pl.ds(h, levels, stride=2), :] = total

        for i in range(4):
            settle(pairs[i][1].at[0], pair_send.at[i])
        settle(weight_in.at[0], weight_send)
        settle(sigma_in, sigma_send)
        settle(flux_sum.at[0], last_send)
        for load in loads[4:]:
            load.wait()

    @pl.when(ocean)
    def _():
        for load in loads[:2]:
            load.wait()
        own = halves(state.at[lev])
        for h in range(2):
            partial = dot(profiles[lev, :, 0], own[h])
            for half in range(2):
                flux_part[half, h] = partial[half * HALF : (half + 1) * HALF]
        remote(
            flux_part.at[1 - lev], flux_half.at[lev], part_send, part_recv, 1, tile, 1 - lev
        )
        remote(adj_hbm, state.at[lev], pair_send.at[0], pair_recv.at[0], 1, tile, 1 - lev)
        flux_half[lev] = flux_part[lev]
        contrib_in[:, :, REACH:] = jnp.zeros((nz, HALF, GROUP - REACH, blk), F32)
        for load in loads[4:]:
            load.wait()
        settle(flux_half.at[0], part_recv)

        totals = [jnp.zeros((HALF, blk), F32) for _ in range(REACH)]
        for r in range(rows):
            flux = flux_half[0, r] + flux_half[1, r]
            flux = jnp.concatenate([flux, jnp.zeros((GROUP - HALF, blk), F32)], axis=0).T
            columns = [jnp.broadcast_to(flux[:, s : s + 1], (blk, blk)) for s in range(HALF)]
            for e in range(NBMAX):
                block = factors[r, e]
                part = jnp.concatenate(
                    [jnp.sum(block * columns[s], axis=0, keepdims=True) for s in range(HALF)],
                    axis=0,
                )
                offset = jnp.where(e < count_ref[r], offs_ref[r, e], -1)
                for b in range(REACH):
                    totals[b] = totals[b] + part * (offset == b).astype(F32)
        for s in range(HALF):
            contrib_in[z, s, :REACH] = jnp.concatenate(
                [totals[b][s : s + 1] for b in range(REACH)], axis=0
            )
        for to in column[:-1]:
            remote(
                contrib_in.at[z, :, pl.ds(0, REACH)],
                contrib_in.at[z, :, pl.ds(0, REACH)],
                contrib_send,
                contrib_recv,
                1,
                to,
                lev,
            )

        size = nz * GROUP
        lane = lax.broadcasted_iota(jnp.int32, (GROUP, size), 1)
        sub = lax.broadcasted_iota(jnp.int32, (GROUP, size), 0)
        place, source = lane % GROUP, lane // GROUP
        have = jnp.zeros((GROUP, size), jnp.int32)
        for i in range(nz):
            have = jnp.where(source == i, match_ref[i * nw + w] - 1, have)
        have = jnp.where(place < REACH, have + place // 2, source * nw + w)
        same = (lane % 2) == (sub % 2)
        picks = []
        for q in range(0, nw, 4):
            wanted = z * nw + q + sub // 2
            hit = jnp.bitwise_and(have - wanted, tiles - 1) == 0
            hit = jnp.logical_and(jnp.logical_and(hit, same), place < REACH)
            picks.append(hit.astype(F32))
        to_atmos = jnp.concatenate(picks, axis=0)[: 2 * nw]
        picks = []
        for q in range(nw):
            wanted = match_ref[z * nw + q] - 1 + sub // 2
            hit = jnp.bitwise_and(have - wanted, tiles - 1) == 0
            hit = jnp.logical_and(jnp.logical_and(hit, same), sub < REACH)
            picks.append(hit.astype(F32))
        to_ocean = jnp.concatenate(picks, axis=0)

        for load in loads[2:4]:
            load.wait()
        settle(state.at[0], pair_recv.at[0])
        first, second = halves(state.at[0]), halves(state.at[1])
        bases = [
            dot(operators[lev, :, 0], jnp.concatenate([first[h], second[h]], axis=0)) for h in range(2)
        ]
        skin_column = jnp.broadcast_to(column_of(skins[lev]), (levels, blk))

        settle(contrib_in.at[: nz - 1, :, pl.ds(0, REACH)], contrib_recv)
        column_data = [contrib_in[:, s].reshape(size, blk) for s in range(HALF)]
        for s in range(HALF):
            picked = dot(to_atmos, column_data[s])
            for q in range(nw):
                flux_out[q, s] = picked[2 * q : 2 * q + 2]
        for k in range(nw):
            remote(
                flux_out.at[steps[k]], flux_in.at[w], flux_send, flux_recv, 0, row[k], lev
            )
        settle(weight_in.at[0], weight_recv)
        total = jnp.zeros((size, blk), F32)
        for s in range(HALF):
            weight = jnp.where(
                lev == 0, weight_in[0, s : s + 1], weight_in[0, HALF + s : HALF + s + 1]
            )
            total = total + weight * column_data[s]
        mixed[...] = total
        settle(sigma_in, sigma_recv)
        for i in range(nz):
            mixed[i * GROUP + REACH : (i + 1) * GROUP] = sigma_in[i]
        heat_out[...] = dot(to_ocean, mixed[...]).reshape(nw, GROUP, blk)
        for k in range(nw - 1):
            remote(
                heat_out.at[steps[k]], heat_in.at[w], heat_send, heat_recv, 1, row[k], lev
            )
        heat_in[w] = heat_out[w]
        settle(heat_in.at[: nw - 1], heat_recv)
        total = heat_in[0]
        for k in range(1, nw):
            total = total + heat_in[k]
        heat_sum[lev] = total
        remote(heat_sum.at[lev], heat_sum.at[lev], last_send, last_recv, 1, tile, 1 - lev)
        settle(heat_sum.at[0], last_recv)
        heat[...] = heat_sum[0] + heat_sum[1]
        for r in range(rows):
            total = jnp.zeros((blk, blk), F32)
            for e in range(NBMAX):
                used = (e < count_ref[r]).astype(F32)
                total = total + factors[r, e] * (heat[pl.ds(offs_ref[r, e], 1), :] * used)
            warmth = lax.dot_general(
                skin_column,
                total,
                (((1,), (1,)), ((), ())),
                precision=HIGHEST,
                preferred_element_type=F32,
            )
            out_ref[pl.ds(r, levels, stride=2), :] = bases[r] + warmth

        settle(flux_part.at[0], part_send)
        settle(state.at[0], pair_send.at[0])
        settle(contrib_in.at[: nz - 1, :, pl.ds(0, REACH)], contrib_send)
        settle(flux_in, flux_send)
        settle(heat_in.at[: nw - 1], heat_send)
        settle(heat_sum.at[0], last_send)


def on_device(
    adj_final,
    flipped_vertical_steppers,
    profiles,
    skin_sensitivity_pair,
    match,
    remap_offs,
    remap_count,
    conserving_transfer_factors,
):
    tiles = lax.axis_size("tile")
    nz = 2 ** ((tiles.bit_length() - 1) // 2)
    nw = tiles // nz
    levels, cells = adj_final.shape[1:]
    rows, _, blk, _ = conserving_transfer_factors.shape
    hbm = pl.BlockSpec(memory_space=pltpu.HBM)
    dma = pltpu.SemaphoreType.DMA
    arrays = (
        match,
        remap_offs,
        remap_count,
        adj_final.reshape(levels * rows, blk),
        flipped_vertical_steppers.reshape(levels, 1, 2 * levels),
        profiles.reshape(STEPS, 1, levels),
        skin_sensitivity_pair,
        conserving_transfer_factors,
    )
    out = pl.pallas_call(
        functools.partial(kernel, nz, nw),
        out_shape=jax.ShapeDtypeStruct((levels * rows, blk), F32),
        in_specs=[hbm] * 8,
        out_specs=pl.BlockSpec(memory_space=pltpu.VMEM),
        scratch_shapes=[
            pltpu.SMEM(match.shape, jnp.int32),
            pltpu.SMEM(remap_offs.shape, jnp.int32),
            pltpu.SMEM(remap_count.shape, jnp.int32),
            pltpu.VMEM((rows, NBMAX, blk, blk), F32),
            pltpu.VMEM((2, levels * rows, blk), F32),
            pltpu.VMEM((2, levels, 1, 2 * levels), F32),
            pltpu.VMEM((2, STEPS, 1, levels), F32),
            pltpu.VMEM((2, 1, levels), F32),
            pltpu.VMEM((2, 2, HALF, blk), F32),
            pltpu.VMEM((2, 2, HALF, blk), F32),
            pltpu.VMEM((nz, HALF, GROUP, blk), F32),
            pltpu.VMEM((2, GROUP, blk), F32),
            pltpu.VMEM((2, blk), F32),
            pltpu.VMEM((nz, 2, blk), F32),
            pltpu.VMEM((nz * GROUP, blk), F32),
            pltpu.VMEM((nw, HALF, 2, blk), F32),
            pltpu.VMEM((nw, HALF, 2, blk), F32),
            pltpu.VMEM((2, HALF, 2, blk), F32),
            pltpu.VMEM((nw, GROUP, blk), F32),
            pltpu.VMEM((nw, GROUP, blk), F32),
            pltpu.VMEM((2, GROUP, blk), F32),
            pltpu.VMEM((GROUP, blk), F32),
            dma((8,)),
            dma((4,)),
            dma((4,)),
        ]
        + [dma] * 14,
        compiler_params=pltpu.CompilerParams(
            has_side_effects=True, collective_id=0, vmem_limit_bytes=32 << 20
        ),
    )(
        *(pltpu.with_memory_space_constraint(array, pltpu.HBM) for array in arrays)
    )
    return out.reshape(1, levels, cells)


def solution(mesh):
    return jax.shard_map(
        on_device,
        mesh=mesh,
        in_specs=(
            P("comp", "lev", "tile"),
            P("comp", "lev", None),
            P("comp", None, "lev"),
            P("comp", "lev"),
            P(),
            P("tile", None),
            P("tile"),
            P("tile", None, None, None),
        ),
        out_specs=P("comp", "lev", "tile"),
        check_vma=False,
    )
```

```python
import functools

import jax
import jax.numpy as jnp
from jax import lax
from jax.experimental import pallas as pl
from jax.experimental.pallas import tpu as pltpu
from jax.sharding import PartitionSpec as P

STEPS = 6
NBMAX = 4
HALF = STEPS // 2
F32 = jnp.float32
HIGHEST = lax.Precision.HIGHEST
MESH = pl.DeviceIdType.MESH
REACH = 6
GROUP = 8


def dot(a, b):
    return jnp.dot(a, b, precision=HIGHEST, preferred_element_type=F32)


def pick(hits, values):
    hits = hits.astype(jnp.bfloat16)
    total = None
    for _ in range(3):
        part = values.astype(jnp.bfloat16)
        values = values - part.astype(F32)
        term = jnp.dot(hits, part, preferred_element_type=F32)
        total = term if total is None else total + term
    return total


def column_of(row):
    n = row.shape[1]
    diagonal = lax.broadcasted_iota(jnp.int32, (n, n), 0) == lax.broadcasted_iota(
        jnp.int32, (n, n), 1
    )
    return jnp.sum(jnp.where(diagonal, row, 0.0), axis=1, keepdims=True)


def kernel(
    nz,
    nw,
    match_hbm,
    offs_hbm,
    count_hbm,
    adj_hbm,
    operator_hbm,
    profile_hbm,
    skin_hbm,
    factors_hbm,
    out_ref,
    match_ref,
    offs_ref,
    count_ref,
    factors,
    state,
    operators,
    profiles,
    skins,
    flux_part,
    flux_half,
    contrib_in,
    weight_in,
    sigma_own,
    sigma_in,
    mixed,
    flux_out,
    flux_in,
    flux_sum,
    heat_out,
    heat_in,
    heat_sum,
    heat,
    load_sem,
    pair_send,
    pair_recv,
    part_send,
    part_recv,
    contrib_send,
    contrib_recv,
    weight_send,
    weight_recv,
    sigma_send,
    sigma_recv,
    flux_send,
    flux_recv,
    heat_send,
    heat_recv,
    last_send,
    last_recv,
):
    comp = lax.axis_index("comp")
    lev = lax.axis_index("lev")
    tile = lax.axis_index("tile")
    tiles = nz * nw
    z = tile // nw
    w = tile % nw
    levels = operators.shape[1]
    blk = factors.shape[2]
    rows = factors.shape[0]
    ny = nw // 2
    far = sorted(range(nz), key=lambda k: -min(k, nz - k))
    column = [((z + k) % nz) * nw + w for k in far]
    far = sorted(
        ((i, k) for i in range(2) for k in range(ny)),
        key=lambda ik: (-min(ik[1], ny - ik[1]), -ik[0]),
    )
    steps = [((w // ny + i) % 2) * ny + (w % ny + k) % ny for i, k in far]
    row = [z * nw + q for q in steps]
    atmos, ocean = comp == 0, comp == 1

    def remote(src, dst, send, recv, to_comp, to_tile, to_lev):
        pltpu.make_async_remote_copy(
            src_ref=src,
            dst_ref=dst,
            send_sem=send,
            recv_sem=recv,
            device_id=(to_comp, to_tile, to_lev),
            device_id_type=MESH,
        ).start()

    def settle(ref, sem):
        pltpu.make_async_copy(ref, ref, sem).wait()

    def halves(ref):
        return [ref[pl.ds(h, levels, stride=2), :] for h in range(2)]

    loads = [
        pltpu.make_async_copy(src, dst, load_sem.at[i])
        for i, (src, dst) in enumerate(
            (
                (adj_hbm, state.at[lev]),
                (profile_hbm, profiles.at[lev]),
                (operator_hbm, operators.at[lev]),
                (skin_hbm, skins.at[lev]),
                (factors_hbm, factors),
                (offs_hbm, offs_ref),
                (count_hbm, count_ref),
                (match_hbm, match_ref),
            )
        )
    ]
    barrier = pltpu.get_barrier_semaphore()

    def greet(to_comp, to_tile, to_lev):
        pl.semaphore_signal(
            barrier, inc=1, device_id=(to_comp, to_tile, to_lev), device_id_type=MESH
        )

    greet(comp, tile, 1 - lev)

    @pl.when(atmos)
    def _():
        for to in row:
            greet(1, to, lev)
        for load in loads:
            load.start()
        for load in loads[:4]:
            load.wait()
        pl.semaphore_wait(barrier, 1 + nz)

    @pl.when(ocean)
    def _():
        for to in column:
            greet(0, to, lev)
        for to in column[:-1] + row[:-1]:
            greet(1, to, lev)
        for load in loads:
            load.start()
        contrib_in[:, :, REACH:] = jnp.zeros((nz, HALF, GROUP - REACH, blk), F32)
        for load in loads[:2] + loads[4:]:
            load.wait()
        own = halves(state.at[lev])
        totals = [jnp.zeros((STEPS, blk), F32) for _ in range(REACH)]
        for r in range(rows):
            flux = dot(profiles[lev, :, 0], own[r])
            flux = jnp.concatenate([flux, jnp.zeros((GROUP - STEPS, blk), F32)], axis=0).T
            columns = [jnp.broadcast_to(flux[:, s : s + 1], (blk, blk)) for s in range(STEPS)]
            for e in range(NBMAX):
                block = factors[r, e]
                part = jnp.concatenate(
                    [jnp.sum(block * columns[s], axis=0, keepdims=True) for s in range(STEPS)],
                    axis=0,
                )
                offset = jnp.where(e < count_ref[r], offs_ref[r, e], -1)
                for b in range(REACH):
                    totals[b] = totals[b] + part * (offset == b).astype(F32)
        for s in range(STEPS):
            flux_part[s // HALF, s % HALF] = jnp.concatenate(
                [totals[b][s : s + 1] for b in range(REACH)], axis=0
            )
        pl.semaphore_wait(barrier, nz + 2 * nw - 1)

    pairs = (state, operators, profiles, skins)

    @pl.when(atmos)
    def _():
        for i in (1, 3, 2, 0):
            ref = pairs[i].at[lev]
            remote(ref, ref, pair_send.at[i], pair_recv.at[i], 0, tile, 1 - lev)
        for i in (1, 2, 3):
            settle(pairs[i].at[0], pair_recv.at[i])
        whole = jnp.concatenate([operators[0, :, 0], operators[1, :, 0]], axis=0)
        profile_rows = jnp.concatenate([profiles[0, :, 0], profiles[1, :, 0]], axis=1)

        first = jnp.concatenate([skins[0], skins[1]], axis=1)
        first = jnp.concatenate([first, dot(first, whole)], axis=0)
        square = dot(whole, whole)
        second = dot(first, square)
        chain = (first, second, dot(second, square))
        total = jnp.zeros((1, 2 * levels), F32)
        for s in range(STEPS):
            total = total + chain[s // 2][s % 2 : s % 2 + 1]
            weight = jnp.sum(total * profile_rows[s : s + 1], axis=1, keepdims=True)
            weight_in[1, s : s + 1] = jnp.broadcast_to(weight, (1, blk))
        remote(weight_in.at[1], weight_in.at[0], weight_send, weight_recv, 1, tile, lev)
        mine = jnp.where(lev == 0, total[:, :levels], total[:, levels:])
        own = halves(state.at[lev])
        for h in range(2):
            sigma_own[h : h + 1] = dot(mine, own[h])
        for to in column:
            remote(sigma_own, sigma_in.at[z], sigma_send, sigma_recv, 1, to, lev)

        power = operators[lev, :, 0]
        shares = []
        for s in range(STEPS):
            if s > 0:
                power = dot(power, whole)
            shares.append(jnp.sum(power * profile_rows[s : s + 1], axis=1, keepdims=True))
        settle(state.at[0], pair_recv.at[0])
        first, second = halves(state.at[0]), halves(state.at[1])
        bases = [dot(power, jnp.concatenate([first[h], second[h]], axis=0)) for h in range(2)]

        settle(flux_in, flux_recv)
        total = flux_in[0]
        for k in range(1, nw):
            total = total + flux_in[k]
        flux_sum[lev] = total
        remote(flux_sum.at[lev], flux_sum.at[lev], last_send, last_recv, 0, tile, 1 - lev)
        settle(flux_sum.at[0], last_recv)
        for h in range(2):
            total = bases[h]
            for s in range(STEPS):
                total = total + shares[s] * flux_sum[s // HALF, s % HALF, h : h + 1]
            out_ref[pl.ds(h, levels, stride=2), :] = total

        for i in range(4):
            settle(pairs[i].at[0], pair_send.at[i])
        settle(weight_in.at[0], weight_send)
        settle(sigma_in, sigma_send)
        settle(flux_sum.at[0], last_send)
        for load in loads[4:]:
            load.wait()

    @pl.when(ocean)
    def _():
        remote(
            flux_part.at[1 - lev], flux_half, part_send, part_recv, 1, tile, 1 - lev
        )
        settle(flux_half, part_recv)
        contrib_in[z, :, :REACH] = flux_part[lev] + flux_half[...]
        for to in column[:-1]:
            remote(
                contrib_in.at[z, :, pl.ds(0, REACH)],
                contrib_in.at[z, :, pl.ds(0, REACH)],
                contrib_send,
                contrib_recv,
                1,
                to,
                lev,
            )

        remote(state.at[lev], state.at[lev], pair_send.at[0], pair_recv.at[0], 1, tile, 1 - lev)

        size = nz * GROUP
        lane = lax.broadcasted_iota(jnp.int32, (GROUP, size), 1)
        sub = lax.broadcasted_iota(jnp.int32, (GROUP, size), 0)
        place, source = lane % GROUP, lane // GROUP
        have = jnp.zeros((GROUP, size), jnp.int32)
        for i in range(nz):
            have = jnp.where(source == i, match_ref[i * nw + w] - 1, have)
        have = jnp.where(place < REACH, have + place // 2, source * nw + w)
        same = (lane % 2) == (sub % 2)
        picks = []
        for q in range(0, nw, 4):
            wanted = z * nw + q + sub // 2
            hit = jnp.bitwise_and(have - wanted, tiles - 1) == 0
            hit = jnp.logical_and(jnp.logical_and(hit, same), place < REACH)
            picks.append(hit.astype(F32))
        to_atmos = jnp.concatenate(picks, axis=0)[: 2 * nw]
        picks = []
        for q in range(nw):
            wanted = match_ref[z * nw + q] - 1 + sub // 2
            hit = jnp.bitwise_and(have - wanted, tiles - 1) == 0
            hit = jnp.logical_and(jnp.logical_and(hit, same), sub < REACH)
            picks.append(hit.astype(F32))
        to_ocean = jnp.concatenate(picks, axis=0)

        for load in loads[2:4]:
            load.wait()
        settle(state.at[0], pair_recv.at[0])
        first, second = halves(state.at[0]), halves(state.at[1])
        bases = [
            dot(operators[lev, :, 0], jnp.concatenate([first[h], second[h]], axis=0)) for h in range(2)
        ]
        skin_column = jnp.broadcast_to(column_of(skins[lev]), (levels, blk))

        settle(contrib_in.at[: nz - 1, :, pl.ds(0, REACH)], contrib_recv)
        column_data = [contrib_in[:, s].reshape(size, blk) for s in range(HALF)]
        for s in range(HALF):
            picked = pick(to_atmos, column_data[s])
            for q in range(nw):
                flux_out[q, s] = picked[2 * q : 2 * q + 2]
        for k in range(nw):
            remote(
                flux_out.at[steps[k]], flux_in.at[w], flux_send, flux_recv, 0, row[k], lev
            )
        settle(weight_in.at[0], weight_recv)
        total = jnp.zeros((size, blk), F32)
        for s in range(HALF):
            weight = jnp.where(
                lev == 0, weight_in[0, s : s + 1], weight_in[0, HALF + s : HALF + s + 1]
            )
            total = total + weight * column_data[s]
        mixed[...] = total
        settle(sigma_in, sigma_recv)
        for i in range(nz):
            mixed[i * GROUP + REACH : (i + 1) * GROUP] = sigma_in[i]
        warm = pick(to_ocean, mixed[...])
        for q in range(nw):
            heat_out[q] = warm[q * GROUP : q * GROUP + REACH]
        for k in range(nw - 1):
            remote(
                heat_out.at[steps[k]], heat_in.at[w], heat_send, heat_recv, 1, row[k], lev
            )
        heat_in[w] = heat_out[w]
        settle(heat_in.at[: nw - 1], heat_recv)
        total = heat_in[0]
        for k in range(1, nw):
            total = total + heat_in[k]
        heat_sum[lev] = total
        remote(heat_sum.at[lev], heat_sum.at[lev], last_send, last_recv, 1, tile, 1 - lev)
        settle(heat_sum.at[0], last_recv)
        heat[...] = heat_sum[0] + heat_sum[1]
        for r in range(rows):
            total = jnp.zeros((blk, blk), F32)
            for e in range(NBMAX):
                used = (e < count_ref[r]).astype(F32)
                total = total + factors[r, e] * (heat[pl.ds(offs_ref[r, e], 1), :] * used)
            warmth = lax.dot_general(
                skin_column,
                total,
                (((1,), (1,)), ((), ())),
                precision=HIGHEST,
                preferred_element_type=F32,
            )
            out_ref[pl.ds(r, levels, stride=2), :] = bases[r] + warmth

        settle(flux_part.at[0], part_send)
        settle(state.at[0], pair_send.at[0])
        settle(contrib_in.at[: nz - 1, :, pl.ds(0, REACH)], contrib_send)
        settle(flux_in, flux_send)
        settle(heat_in.at[: nw - 1], heat_send)
        settle(heat_sum.at[0], last_send)


def on_device(
    adj_final,
    flipped_vertical_steppers,
    profiles,
    skin_sensitivity_pair,
    match,
    remap_offs,
    remap_count,
    conserving_transfer_factors,
):
    tiles = lax.axis_size("tile")
    nz = 2 ** ((tiles.bit_length() - 1) // 2)
    nw = tiles // nz
    levels, cells = adj_final.shape[1:]
    rows, _, blk, _ = conserving_transfer_factors.shape
    hbm = pl.BlockSpec(memory_space=pltpu.HBM)
    dma = pltpu.SemaphoreType.DMA
    arrays = (
        match,
        remap_offs,
        remap_count,
        adj_final.reshape(levels * rows, blk),
        flipped_vertical_steppers.reshape(levels, 1, 2 * levels),
        profiles.reshape(STEPS, 1, levels),
        skin_sensitivity_pair,
        conserving_transfer_factors,
    )
    out = pl.pallas_call(
        functools.partial(kernel, nz, nw),
        out_shape=jax.ShapeDtypeStruct((levels * rows, blk), F32),
        in_specs=[hbm] * 8,
        out_specs=pl.BlockSpec(memory_space=pltpu.VMEM),
        scratch_shapes=[
            pltpu.SMEM(match.shape, jnp.int32),
            pltpu.SMEM(remap_offs.shape, jnp.int32),
            pltpu.SMEM(remap_count.shape, jnp.int32),
            pltpu.VMEM((rows, NBMAX, blk, blk), F32),
            pltpu.VMEM((2, levels * rows, blk), F32),
            pltpu.VMEM((2, levels, 1, 2 * levels), F32),
            pltpu.VMEM((2, STEPS, 1, levels), F32),
            pltpu.VMEM((2, 1, levels), F32),
            pltpu.VMEM((2, HALF, REACH, blk), F32),
            pltpu.VMEM((HALF, REACH, blk), F32),
            pltpu.VMEM((nz, HALF, GROUP, blk), F32),
            pltpu.VMEM((2, GROUP, blk), F32),
            pltpu.VMEM((2, blk), F32),
            pltpu.VMEM((nz, 2, blk), F32),
            pltpu.VMEM((nz * GROUP, blk), F32),
            pltpu.VMEM((nw, HALF, 2, blk), F32),
            pltpu.VMEM((nw, HALF, 2, blk), F32),
            pltpu.VMEM((2, HALF, 2, blk), F32),
            pltpu.VMEM((nw, REACH, blk), F32),
            pltpu.VMEM((nw, REACH, blk), F32),
            pltpu.VMEM((2, REACH, blk), F32),
            pltpu.VMEM((REACH, blk), F32),
            dma((8,)),
            dma((4,)),
            dma((4,)),
        ]
        + [dma] * 14,
        compiler_params=pltpu.CompilerParams(
            has_side_effects=True, collective_id=0, vmem_limit_bytes=32 << 20
        ),
    )(
        *(pltpu.with_memory_space_constraint(array, pltpu.HBM) for array in arrays)
    )
    return out.reshape(1, levels, cells)


def solution(mesh):
    return jax.shard_map(
        on_device,
        mesh=mesh,
        in_specs=(
            P("comp", "lev", "tile"),
            P("comp", "lev", None),
            P("comp", None, "lev"),
            P("comp", "lev"),
            P(),
            P("tile", None),
            P("tile"),
            P("tile", None, None, None),
        ),
        out_specs=P("comp", "lev", "tile"),
        check_vma=False,
    )
```

```python
import functools

import jax
import jax.numpy as jnp
from jax import lax
from jax.experimental import pallas as pl
from jax.experimental.pallas import tpu as pltpu
from jax.sharding import PartitionSpec as P

STEPS = 6
NBMAX = 4
HALF = STEPS // 2
F32 = jnp.float32
HIGHEST = lax.Precision.HIGHEST
MESH = pl.DeviceIdType.MESH
REACH = 6
GROUP = 8


def dot(a, b):
    return jnp.dot(a, b, precision=HIGHEST, preferred_element_type=F32)


def pick(hits, values):
    hits = hits.astype(jnp.bfloat16)
    total = None
    for _ in range(3):
        part = values.astype(jnp.bfloat16)
        values = values - part.astype(F32)
        term = jnp.dot(hits, part, preferred_element_type=F32)
        total = term if total is None else total + term
    return total


def column_of(row):
    n = row.shape[1]
    diagonal = lax.broadcasted_iota(jnp.int32, (n, n), 0) == lax.broadcasted_iota(
        jnp.int32, (n, n), 1
    )
    return jnp.sum(jnp.where(diagonal, row, 0.0), axis=1, keepdims=True)


def kernel(
    nz,
    nw,
    match_hbm,
    offs_hbm,
    count_hbm,
    adj_hbm,
    operator_hbm,
    profile_hbm,
    skin_hbm,
    factors_hbm,
    out_ref,
    match_ref,
    offs_ref,
    count_ref,
    factors,
    state,
    operators,
    profiles,
    skins,
    flux_part,
    flux_half,
    contrib_in,
    weight_in,
    sigma_own,
    sigma_in,
    mixed,
    flux_out,
    flux_in,
    flux_sum,
    heat_out,
    heat_in,
    heat_sum,
    heat,
    load_sem,
    pair_send,
    pair_recv,
    part_send,
    part_recv,
    contrib_send,
    contrib_recv,
    weight_send,
    weight_recv,
    sigma_send,
    sigma_recv,
    flux_send,
    flux_recv,
    heat_send,
    heat_recv,
    last_send,
    last_recv,
):
    comp = lax.axis_index("comp")
    lev = lax.axis_index("lev")
    tile = lax.axis_index("tile")
    tiles = nz * nw
    z = tile // nw
    w = tile % nw
    levels = operators.shape[1]
    blk = factors.shape[2]
    rows = factors.shape[0]
    ny = nw // 2
    far = sorted(range(nz), key=lambda k: -min(k, nz - k))
    column = [((z + k) % nz) * nw + w for k in far]
    far = sorted(
        ((i, k) for i in range(2) for k in range(ny)),
        key=lambda ik: (-min(ik[1], ny - ik[1]), -ik[0]),
    )
    steps = [((w // ny + i) % 2) * ny + (w % ny + k) % ny for i, k in far]
    row = [z * nw + q for q in steps]
    atmos, ocean = comp == 0, comp == 1

    def remote(src, dst, send, recv, to_comp, to_tile, to_lev):
        pltpu.make_async_remote_copy(
            src_ref=src,
            dst_ref=dst,
            send_sem=send,
            recv_sem=recv,
            device_id=(to_comp, to_tile, to_lev),
            device_id_type=MESH,
        ).start()

    def settle(ref, sem):
        pltpu.make_async_copy(ref, ref, sem).wait()

    def halves(ref):
        return [ref[pl.ds(h, levels, stride=2), :] for h in range(2)]

    loads = [
        pltpu.make_async_copy(src, dst, load_sem.at[i])
        for i, (src, dst) in enumerate(
            (
                (adj_hbm, state.at[lev]),
                (profile_hbm, profiles.at[lev]),
                (operator_hbm, operators.at[lev]),
                (skin_hbm, skins.at[lev]),
                (factors_hbm, factors),
                (offs_hbm, offs_ref),
                (count_hbm, count_ref),
                (match_hbm, match_ref),
            )
        )
    ]
    barrier = pltpu.get_barrier_semaphore()

    def greet(to_comp, to_tile, to_lev):
        pl.semaphore_signal(
            barrier, inc=1, device_id=(to_comp, to_tile, to_lev), device_id_type=MESH
        )

    greet(comp, tile, 1 - lev)

    @pl.when(atmos)
    def _():
        for to in row:
            greet(1, to, lev)
        for load in loads:
            load.start()
        for load in loads[:4]:
            load.wait()
        pl.semaphore_wait(barrier, 1 + nz)

    @pl.when(ocean)
    def _():
        for to in row[:-1] + column[:-1]:
            greet(1, to, lev)
        for to in column:
            greet(0, to, lev)
        for load in loads:
            load.start()
        contrib_in[:, :, REACH:] = jnp.zeros((nz, HALF, GROUP - REACH, blk), F32)
        for load in loads[:2] + loads[4:]:
            load.wait()
        own = halves(state.at[lev])
        totals = [jnp.zeros((STEPS, blk), F32) for _ in range(REACH)]
        for r in range(rows):
            flux = dot(profiles[lev, :, 0], own[r])
            flux = jnp.concatenate([flux, jnp.zeros((GROUP - STEPS, blk), F32)], axis=0).T
            columns = [jnp.broadcast_to(flux[:, s : s + 1], (blk, blk)) for s in range(STEPS)]
            for e in range(NBMAX):
                block = factors[r, e]
                part = jnp.concatenate(
                    [jnp.sum(block * columns[s], axis=0, keepdims=True) for s in range(STEPS)],
                    axis=0,
                )
                offset = jnp.where(e < count_ref[r], offs_ref[r, e], -1)
                for b in range(REACH):
                    totals[b] = totals[b] + part * (offset == b).astype(F32)
        for s in range(STEPS):
            flux_part[s // HALF, s % HALF] = jnp.concatenate(
                [totals[b][s : s + 1] for b in range(REACH)], axis=0
            )
        pl.semaphore_wait(barrier, nz + 2 * nw - 1)

    pairs = (state, operators, profiles, skins)

    @pl.when(atmos)
    def _():
        for i in (1, 3, 2):
            ref = pairs[i].at[lev]
            remote(ref, ref, pair_send.at[i], pair_recv.at[i], 0, tile, 1 - lev)
        for i in (1, 2, 3):
            settle(pairs[i].at[0], pair_recv.at[i])
        whole = jnp.concatenate([operators[0, :, 0], operators[1, :, 0]], axis=0)
        profile_rows = jnp.concatenate([profiles[0, :, 0], profiles[1, :, 0]], axis=1)

        first = jnp.concatenate([skins[0], skins[1]], axis=1)
        first = jnp.concatenate([first, dot(first, whole)], axis=0)
        square = dot(whole, whole)
        second = dot(first, square)
        chain = (first, second, dot(second, square))
        total = jnp.zeros((1, 2 * levels), F32)
        for s in range(STEPS):
            total = total + chain[s // 2][s % 2 : s % 2 + 1]
            weight = jnp.sum(total * profile_rows[s : s + 1], axis=1, keepdims=True)
            weight_in[1, s : s + 1] = jnp.broadcast_to(weight, (1, blk))
        remote(weight_in.at[1], weight_in.at[0], weight_send, weight_recv, 1, tile, lev)
        mine = jnp.where(lev == 0, total[:, :levels], total[:, levels:])
        own = halves(state.at[lev])
        for h in range(2):
            sigma_own[h : h + 1] = dot(mine, own[h])
        for to in column:
            remote(sigma_own, sigma_in.at[z], sigma_send, sigma_recv, 1, to, lev)
        ref = state.at[lev]
        remote(ref, ref, pair_send.at[0], pair_recv.at[0], 0, tile, 1 - lev)

        power = operators[lev, :, 0]
        shares = []
        for s in range(STEPS):
            if s > 0:
                power = dot(power, whole)
            shares.append(jnp.sum(power * profile_rows[s : s + 1], axis=1, keepdims=True))
        settle(state.at[0], pair_recv.at[0])
        first, second = halves(state.at[0]), halves(state.at[1])
        bases = [dot(power, jnp.concatenate([first[h], second[h]], axis=0)) for h in range(2)]

        settle(flux_in, flux_recv)
        total = flux_in[0]
        for k in range(1, nw):
            total = total + flux_in[k]
        flux_sum[lev] = total
        remote(flux_sum.at[lev], flux_sum.at[lev], last_send, last_recv, 0, tile, 1 - lev)
        settle(flux_sum.at[0], last_recv)
        for h in range(2):
            total = bases[h]
            for s in range(STEPS):
                total = total + shares[s] * flux_sum[s // HALF, s % HALF, h : h + 1]
            out_ref[pl.ds(h, levels, stride=2), :] = total

        for i in range(4):
            settle(pairs[i].at[0], pair_send.at[i])
        settle(weight_in.at[0], weight_send)
        settle(sigma_in, sigma_send)
        settle(flux_sum.at[0], last_send)
        for load in loads[4:]:
            load.wait()

    @pl.when(ocean)
    def _():
        remote(
            flux_part.at[1 - lev], flux_half, part_send, part_recv, 1, tile, 1 - lev
        )
        settle(flux_half, part_recv)
        contrib_in[z, :, :REACH] = flux_part[lev] + flux_half[...]
        for to in column[:-1]:
            remote(
                contrib_in.at[z, :, pl.ds(0, REACH)],
                contrib_in.at[z, :, pl.ds(0, REACH)],
                contrib_send,
                contrib_recv,
                1,
                to,
                lev,
            )

        remote(state.at[lev], state.at[lev], pair_send.at[0], pair_recv.at[0], 1, tile, 1 - lev)

        size = nz * GROUP
        lane = lax.broadcasted_iota(jnp.int32, (GROUP, size), 1)
        sub = lax.broadcasted_iota(jnp.int32, (GROUP, size), 0)
        place, source = lane % GROUP, lane // GROUP
        have = jnp.zeros((GROUP, size), jnp.int32)
        for i in range(nz):
            have = jnp.where(source == i, match_ref[i * nw + w] - 1, have)
        have = jnp.where(place < REACH, have + place // 2, source * nw + w)
        same = (lane % 2) == (sub % 2)
        picks = []
        for q in range(0, nw, 4):
            wanted = z * nw + q + sub // 2
            hit = jnp.bitwise_and(have - wanted, tiles - 1) == 0
            hit = jnp.logical_and(jnp.logical_and(hit, same), place < REACH)
            picks.append(hit.astype(F32))
        to_atmos = jnp.concatenate(picks, axis=0)[: 2 * nw]
        picks = []
        for q in range(nw):
            wanted = match_ref[z * nw + q] - 1 + sub // 2
            hit = jnp.bitwise_and(have - wanted, tiles - 1) == 0
            hit = jnp.logical_and(jnp.logical_and(hit, same), sub < REACH)
            picks.append(hit.astype(F32))
        to_ocean = jnp.concatenate(picks, axis=0)

        settle(contrib_in.at[: nz - 1, :, pl.ds(0, REACH)], contrib_recv)
        column_data = [contrib_in[:, s].reshape(size, blk) for s in range(HALF)]
        for s in range(HALF):
            picked = pick(to_atmos, column_data[s])
            for q in range(nw):
                flux_out[q, s] = picked[2 * q : 2 * q + 2]
        for k in range(nw):
            remote(
                flux_out.at[steps[k]], flux_in.at[w], flux_send, flux_recv, 0, row[k], lev
            )
        settle(weight_in.at[0], weight_recv)
        total = jnp.zeros((size, blk), F32)
        for s in range(HALF):
            weight = jnp.where(
                lev == 0, weight_in[0, s : s + 1], weight_in[0, HALF + s : HALF + s + 1]
            )
            total = total + weight * column_data[s]
        mixed[...] = total
        settle(sigma_in, sigma_recv)
        for i in range(nz):
            mixed[i * GROUP + REACH : (i + 1) * GROUP] = sigma_in[i]
        warm = pick(to_ocean, mixed[...])
        for q in range(nw):
            heat_out[q] = warm[q * GROUP : q * GROUP + REACH]
        for k in range(nw - 1):
            remote(
                heat_out.at[steps[k]], heat_in.at[w], heat_send, heat_recv, 1, row[k], lev
            )
        for load in loads[2:4]:
            load.wait()
        settle(state.at[0], pair_recv.at[0])
        first, second = halves(state.at[0]), halves(state.at[1])
        bases = [
            dot(operators[lev, :, 0], jnp.concatenate([first[h], second[h]], axis=0)) for h in range(2)
        ]
        skin_column = jnp.broadcast_to(column_of(skins[lev]), (levels, blk))

        heat_in[w] = heat_out[w]
        settle(heat_in.at[: nw - 1], heat_recv)
        total = heat_in[0]
        for k in range(1, nw):
            total = total + heat_in[k]
        heat_sum[lev] = total
        remote(heat_sum.at[lev], heat_sum.at[lev], last_send, last_recv, 1, tile, 1 - lev)
        settle(heat_sum.at[0], last_recv)
        heat[...] = heat_sum[0] + heat_sum[1]
        for r in range(rows):
            total = jnp.zeros((blk, blk), F32)
            for e in range(NBMAX):
                used = (e < count_ref[r]).astype(F32)
                total = total + factors[r, e] * (heat[pl.ds(offs_ref[r, e], 1), :] * used)
            warmth = lax.dot_general(
                skin_column,
                total,
                (((1,), (1,)), ((), ())),
                precision=HIGHEST,
                preferred_element_type=F32,
            )
            out_ref[pl.ds(r, levels, stride=2), :] = bases[r] + warmth

        settle(flux_part.at[0], part_send)
        settle(state.at[0], pair_send.at[0])
        settle(contrib_in.at[: nz - 1, :, pl.ds(0, REACH)], contrib_send)
        settle(flux_in, flux_send)
        settle(heat_in.at[: nw - 1], heat_send)
        settle(heat_sum.at[0], last_send)


def on_device(
    adj_final,
    flipped_vertical_steppers,
    profiles,
    skin_sensitivity_pair,
    match,
    remap_offs,
    remap_count,
    conserving_transfer_factors,
):
    tiles = lax.axis_size("tile")
    nz = 2 ** ((tiles.bit_length() - 1) // 2)
    nw = tiles // nz
    levels, cells = adj_final.shape[1:]
    rows, _, blk, _ = conserving_transfer_factors.shape
    hbm = pl.BlockSpec(memory_space=pltpu.HBM)
    dma = pltpu.SemaphoreType.DMA
    arrays = (
        match,
        remap_offs,
        remap_count,
        adj_final.reshape(levels * rows, blk),
        flipped_vertical_steppers.reshape(levels, 1, 2 * levels),
        profiles.reshape(STEPS, 1, levels),
        skin_sensitivity_pair,
        conserving_transfer_factors,
    )
    out = pl.pallas_call(
        functools.partial(kernel, nz, nw),
        out_shape=jax.ShapeDtypeStruct((levels * rows, blk), F32),
        in_specs=[hbm] * 8,
        out_specs=pl.BlockSpec(memory_space=pltpu.VMEM),
        scratch_shapes=[
            pltpu.SMEM(match.shape, jnp.int32),
            pltpu.SMEM(remap_offs.shape, jnp.int32),
            pltpu.SMEM(remap_count.shape, jnp.int32),
            pltpu.VMEM((rows, NBMAX, blk, blk), F32),
            pltpu.VMEM((2, levels * rows, blk), F32),
            pltpu.VMEM((2, levels, 1, 2 * levels), F32),
            pltpu.VMEM((2, STEPS, 1, levels), F32),
            pltpu.VMEM((2, 1, levels), F32),
            pltpu.VMEM((2, HALF, REACH, blk), F32),
            pltpu.VMEM((HALF, REACH, blk), F32),
            pltpu.VMEM((nz, HALF, GROUP, blk), F32),
            pltpu.VMEM((2, GROUP, blk), F32),
            pltpu.VMEM((2, blk), F32),
            pltpu.VMEM((nz, 2, blk), F32),
            pltpu.VMEM((nz * GROUP, blk), F32),
            pltpu.VMEM((nw, HALF, 2, blk), F32),
            pltpu.VMEM((nw, HALF, 2, blk), F32),
            pltpu.VMEM((2, HALF, 2, blk), F32),
            pltpu.VMEM((nw, REACH, blk), F32),
            pltpu.VMEM((nw, REACH, blk), F32),
            pltpu.VMEM((2, REACH, blk), F32),
            pltpu.VMEM((REACH, blk), F32),
            dma((8,)),
            dma((4,)),
            dma((4,)),
        ]
        + [dma] * 14,
        compiler_params=pltpu.CompilerParams(
            has_side_effects=True, collective_id=0, vmem_limit_bytes=32 << 20
        ),
    )(
        *(pltpu.with_memory_space_constraint(array, pltpu.HBM) for array in arrays)
    )
    return out.reshape(1, levels, cells)


def solution(mesh):
    return jax.shard_map(
        on_device,
        mesh=mesh,
        in_specs=(
            P("comp", "lev", "tile"),
            P("comp", "lev", None),
            P("comp", None, "lev"),
            P("comp", "lev"),
            P(),
            P("tile", None),
            P("tile"),
            P("tile", None, None, None),
        ),
        out_specs=P("comp", "lev", "tile"),
        check_vma=False,
    )
```

```python
import functools

import jax
import jax.numpy as jnp
from jax import lax
from jax.experimental import pallas as pl
from jax.experimental.pallas import tpu as pltpu
from jax.sharding import PartitionSpec as P

STEPS = 6
NBMAX = 4
HALF = STEPS // 2
F32 = jnp.float32
HIGHEST = lax.Precision.HIGHEST
MESH = pl.DeviceIdType.MESH
REACH = 6
GROUP = 8


def dot(a, b):
    return jnp.dot(a, b, precision=HIGHEST, preferred_element_type=F32)


def pick(hits, values):
    hits = hits.astype(jnp.bfloat16)
    total = None
    for _ in range(3):
        part = values.astype(jnp.bfloat16)
        values = values - part.astype(F32)
        term = jnp.dot(hits, part, preferred_element_type=F32)
        total = term if total is None else total + term
    return total


def column_of(row):
    n = row.shape[1]
    diagonal = lax.broadcasted_iota(jnp.int32, (n, n), 0) == lax.broadcasted_iota(
        jnp.int32, (n, n), 1
    )
    return jnp.sum(jnp.where(diagonal, row, 0.0), axis=1, keepdims=True)


def kernel(
    nz,
    nw,
    match_hbm,
    offs_hbm,
    count_hbm,
    adj_hbm,
    operator_hbm,
    profile_hbm,
    skin_hbm,
    factors_hbm,
    out_ref,
    match_ref,
    offs_ref,
    count_ref,
    factors,
    state,
    operators,
    profiles,
    skins,
    flux_part,
    flux_half,
    contrib_in,
    weight_in,
    sigma_own,
    sigma_in,
    mixed,
    flux_out,
    flux_in,
    flux_sum,
    heat_out,
    heat_in,
    heat_sum,
    heat,
    load_sem,
    pair_send,
    pair_recv,
    part_send,
    part_recv,
    contrib_send,
    contrib_recv,
    weight_send,
    weight_recv,
    sigma_send,
    sigma_recv,
    flux_send,
    flux_recv,
    heat_send,
    heat_recv,
    last_send,
    last_recv,
):
    comp = lax.axis_index("comp")
    lev = lax.axis_index("lev")
    tile = lax.axis_index("tile")
    tiles = nz * nw
    z = tile // nw
    w = tile % nw
    levels = operators.shape[1]
    blk = factors.shape[2]
    rows = factors.shape[0]
    ny = nw // 2
    far = sorted(range(nz), key=lambda k: -min(k, nz - k))
    column = [((z + k) % nz) * nw + w for k in far]
    far = sorted(
        ((i, k) for i in range(2) for k in range(ny)),
        key=lambda ik: (-min(ik[1], ny - ik[1]), -ik[0]),
    )
    steps = [((w // ny + i) % 2) * ny + (w % ny + k) % ny for i, k in far]
    row = [z * nw + q for q in steps]
    atmos, ocean = comp == 0, comp == 1

    def remote(src, dst, send, recv, to_comp, to_tile, to_lev):
        pltpu.make_async_remote_copy(
            src_ref=src,
            dst_ref=dst,
            send_sem=send,
            recv_sem=recv,
            device_id=(to_comp, to_tile, to_lev),
            device_id_type=MESH,
        ).start()

    def settle(ref, sem):
        pltpu.make_async_copy(ref, ref, sem).wait()

    def halves(ref):
        return [ref[pl.ds(h, levels, stride=2), :] for h in range(2)]

    loads = [
        pltpu.make_async_copy(src, dst, load_sem.at[i])
        for i, (src, dst) in enumerate(
            (
                (adj_hbm, state.at[lev]),
                (profile_hbm, profiles.at[lev]),
                (operator_hbm, operators.at[lev]),
                (skin_hbm, skins.at[lev]),
                (factors_hbm, factors),
                (offs_hbm, offs_ref),
                (count_hbm, count_ref),
                (match_hbm, match_ref),
            )
        )
    ]
    barrier = pltpu.get_barrier_semaphore()

    def greet(to_comp, to_tile, to_lev):
        pl.semaphore_signal(
            barrier, inc=1, device_id=(to_comp, to_tile, to_lev), device_id_type=MESH
        )

    greet(comp, tile, 1 - lev)

    @pl.when(atmos)
    def _():
        for to in row:
            greet(1, to, lev)
        for load in loads:
            load.start()
        for load in loads[:4]:
            load.wait()
        pl.semaphore_wait(barrier, 1 + nz)

    @pl.when(ocean)
    def _():
        for to in row[:-1] + column[:-1]:
            greet(1, to, lev)
        for to in column:
            greet(0, to, lev)
        for load in loads:
            load.start()
        contrib_in[:, :, REACH:] = jnp.zeros((nz, HALF, GROUP - REACH, blk), F32)
        for load in loads[:2] + loads[4:]:
            load.wait()
        own = halves(state.at[lev])
        totals = [jnp.zeros((STEPS, blk), F32) for _ in range(REACH)]
        for r in range(rows):
            flux = dot(profiles[lev, :, 0], own[r])
            flux = jnp.concatenate([flux, jnp.zeros((GROUP - STEPS, blk), F32)], axis=0).T
            columns = [jnp.broadcast_to(flux[:, s : s + 1], (blk, blk)) for s in range(STEPS)]
            for e in range(NBMAX):
                block = factors[r, e]
                part = jnp.concatenate(
                    [jnp.sum(block * columns[s], axis=0, keepdims=True) for s in range(STEPS)],
                    axis=0,
                )
                offset = jnp.where(e < count_ref[r], offs_ref[r, e], -1)
                for b in range(REACH):
                    totals[b] = totals[b] + part * (offset == b).astype(F32)
        for s in range(STEPS):
            flux_part[s // HALF, s % HALF] = jnp.concatenate(
                [totals[b][s : s + 1] for b in range(REACH)], axis=0
            )
        pl.semaphore_wait(barrier, nz + 2 * nw - 1)

    pairs = (state, operators, profiles, skins)

    @pl.when(atmos)
    def _():
        for i in (1, 3, 2):
            ref = pairs[i].at[lev]
            remote(ref, ref, pair_send.at[i], pair_recv.at[i], 0, tile, 1 - lev)
        for i in (1, 2, 3):
            settle(pairs[i].at[0], pair_recv.at[i])
        whole = jnp.concatenate([operators[0, :, 0], operators[1, :, 0]], axis=0)
        profile_rows = jnp.concatenate([profiles[0, :, 0], profiles[1, :, 0]], axis=1)

        first = jnp.concatenate([skins[0], skins[1]], axis=1)
        first = jnp.concatenate([first, dot(first, whole)], axis=0)
        square = dot(whole, whole)
        second = dot(first, square)
        chain = (first, second, dot(second, square))
        total = jnp.zeros((1, 2 * levels), F32)
        for s in range(STEPS):
            total = total + chain[s // 2][s % 2 : s % 2 + 1]
            weight = jnp.sum(total * profile_rows[s : s + 1], axis=1, keepdims=True)
            weight_in[1, s : s + 1] = jnp.broadcast_to(weight, (1, blk))
        remote(weight_in.at[1], weight_in.at[0], weight_send, weight_recv, 1, tile, lev)
        mine = jnp.where(lev == 0, total[:, :levels], total[:, levels:])
        own = halves(state.at[lev])
        for h in range(2):
            sigma_own[h : h + 1] = dot(mine, own[h])
        for to in column:
            remote(sigma_own, sigma_in.at[z], sigma_send, sigma_recv, 1, to, lev)
        ref = state.at[lev]
        remote(ref, ref, pair_send.at[0], pair_recv.at[0], 0, tile, 1 - lev)

        mine = operators[lev, :, 0]
        flux_columns = jnp.concatenate(
            [profile_rows, jnp.zeros((GROUP - STEPS, 2 * levels), F32)], axis=0
        ).T
        shares = []
        for s in range(STEPS):
            if s > 0:
                flux_columns = dot(whole, flux_columns)
            shares.append(dot(mine, flux_columns)[:, s : s + 1])
        settle(state.at[0], pair_recv.at[0])
        first, second = halves(state.at[0]), halves(state.at[1])
        bases = []
        for h in range(2):
            moved = jnp.concatenate([first[h], second[h]], axis=0)
            for _ in range(STEPS - 1):
                moved = dot(whole, moved)
            bases.append(dot(mine, moved))

        settle(flux_in, flux_recv)
        total = flux_in[0]
        for k in range(1, nw):
            total = total + flux_in[k]
        flux_sum[lev] = total
        remote(flux_sum.at[lev], flux_sum.at[lev], last_send, last_recv, 0, tile, 1 - lev)
        settle(flux_sum.at[0], last_recv)
        for h in range(2):
            total = bases[h]
            for s in range(STEPS):
                total = total + shares[s] * flux_sum[s // HALF, s % HALF, h : h + 1]
            out_ref[pl.ds(h, levels, stride=2), :] = total

        for i in range(4):
            settle(pairs[i].at[0], pair_send.at[i])
        settle(weight_in.at[0], weight_send)
        settle(sigma_in, sigma_send)
        settle(flux_sum.at[0], last_send)
        for load in loads[4:]:
            load.wait()

    @pl.when(ocean)
    def _():
        remote(
            flux_part.at[1 - lev], flux_half, part_send, part_recv, 1, tile, 1 - lev
        )
        settle(flux_half, part_recv)
        contrib_in[z, :, :REACH] = flux_part[lev] + flux_half[...]
        for to in column[:-1]:
            remote(
                contrib_in.at[z, :, pl.ds(0, REACH)],
                contrib_in.at[z, :, pl.ds(0, REACH)],
                contrib_send,
                contrib_recv,
                1,
                to,
                lev,
            )

        remote(state.at[lev], state.at[lev], pair_send.at[0], pair_recv.at[0], 1, tile, 1 - lev)

        size = nz * GROUP
        lane = lax.broadcasted_iota(jnp.int32, (GROUP, size), 1)
        sub = lax.broadcasted_iota(jnp.int32, (GROUP, size), 0)
        place, source = lane % GROUP, lane // GROUP
        have = jnp.zeros((GROUP, size), jnp.int32)
        for i in range(nz):
            have = jnp.where(source == i, match_ref[i * nw + w] - 1, have)
        have = jnp.where(place < REACH, have + place // 2, source * nw + w)
        same = (lane % 2) == (sub % 2)
        picks = []
        for q in range(0, nw, 4):
            wanted = z * nw + q + sub // 2
            hit = jnp.bitwise_and(have - wanted, tiles - 1) == 0
            hit = jnp.logical_and(jnp.logical_and(hit, same), place < REACH)
            picks.append(hit.astype(F32))
        to_atmos = jnp.concatenate(picks, axis=0)[: 2 * nw]
        picks = []
        for q in range(nw):
            wanted = match_ref[z * nw + q] - 1 + sub // 2
            hit = jnp.bitwise_and(have - wanted, tiles - 1) == 0
            hit = jnp.logical_and(jnp.logical_and(hit, same), sub < REACH)
            picks.append(hit.astype(F32))
        to_ocean = jnp.concatenate(picks, axis=0)

        settle(contrib_in.at[: nz - 1, :, pl.ds(0, REACH)], contrib_recv)
        column_data = [contrib_in[:, s].reshape(size, blk) for s in range(HALF)]
        for s in range(HALF):
            picked = pick(to_atmos, column_data[s])
            for q in range(nw):
                flux_out[q, s] = picked[2 * q : 2 * q + 2]
        for k in range(nw):
            remote(
                flux_out.at[steps[k]], flux_in.at[w], flux_send, flux_recv, 0, row[k], lev
            )
        settle(weight_in.at[0], weight_recv)
        total = jnp.zeros((size, blk), F32)
        for s in range(HALF):
            weight = jnp.where(
                lev == 0, weight_in[0, s : s + 1], weight_in[0, HALF + s : HALF + s + 1]
            )
            total = total + weight * column_data[s]
        mixed[...] = total
        settle(sigma_in, sigma_recv)
        for i in range(nz):
            mixed[i * GROUP + REACH : (i + 1) * GROUP] = sigma_in[i]
        warm = pick(to_ocean, mixed[...])
        for q in range(nw):
            heat_out[q] = warm[q * GROUP : q * GROUP + REACH]
        for k in range(nw - 1):
            remote(
                heat_out.at[steps[k]], heat_in.at[w], heat_send, heat_recv, 1, row[k], lev
            )
        for load in loads[2:4]:
            load.wait()
        settle(state.at[0], pair_recv.at[0])
        first, second = halves(state.at[0]), halves(state.at[1])
        bases = [
            dot(operators[lev, :, 0], jnp.concatenate([first[h], second[h]], axis=0)) for h in range(2)
        ]
        skin_column = jnp.broadcast_to(column_of(skins[lev]), (levels, blk))

        heat_in[w] = heat_out[w]
        settle(heat_in.at[: nw - 1], heat_recv)
        total = heat_in[0]
        for k in range(1, nw):
            total = total + heat_in[k]
        heat_sum[lev] = total
        remote(heat_sum.at[lev], heat_sum.at[lev], last_send, last_recv, 1, tile, 1 - lev)
        settle(heat_sum.at[0], last_recv)
        heat[...] = heat_sum[0] + heat_sum[1]
        for r in range(rows):
            total = jnp.zeros((blk, blk), F32)
            for e in range(NBMAX):
                used = (e < count_ref[r]).astype(F32)
                total = total + factors[r, e] * (heat[pl.ds(offs_ref[r, e], 1), :] * used)
            warmth = lax.dot_general(
                skin_column,
                total,
                (((1,), (1,)), ((), ())),
                precision=HIGHEST,
                preferred_element_type=F32,
            )
            out_ref[pl.ds(r, levels, stride=2), :] = bases[r] + warmth

        settle(flux_part.at[0], part_send)
        settle(state.at[0], pair_send.at[0])
        settle(contrib_in.at[: nz - 1, :, pl.ds(0, REACH)], contrib_send)
        settle(flux_in, flux_send)
        settle(heat_in.at[: nw - 1], heat_send)
        settle(heat_sum.at[0], last_send)


def on_device(
    adj_final,
    flipped_vertical_steppers,
    profiles,
    skin_sensitivity_pair,
    match,
    remap_offs,
    remap_count,
    conserving_transfer_factors,
):
    tiles = lax.axis_size("tile")
    nz = 2 ** ((tiles.bit_length() - 1) // 2)
    nw = tiles // nz
    levels, cells = adj_final.shape[1:]
    rows, _, blk, _ = conserving_transfer_factors.shape
    hbm = pl.BlockSpec(memory_space=pltpu.HBM)
    dma = pltpu.SemaphoreType.DMA
    arrays = (
        match,
        remap_offs,
        remap_count,
        adj_final.reshape(levels * rows, blk),
        flipped_vertical_steppers.reshape(levels, 1, 2 * levels),
        profiles.reshape(STEPS, 1, levels),
        skin_sensitivity_pair,
        conserving_transfer_factors,
    )
    out = pl.pallas_call(
        functools.partial(kernel, nz, nw),
        out_shape=jax.ShapeDtypeStruct((levels * rows, blk), F32),
        in_specs=[hbm] * 8,
        out_specs=pl.BlockSpec(memory_space=pltpu.VMEM),
        scratch_shapes=[
            pltpu.SMEM(match.shape, jnp.int32),
            pltpu.SMEM(remap_offs.shape, jnp.int32),
            pltpu.SMEM(remap_count.shape, jnp.int32),
            pltpu.VMEM((rows, NBMAX, blk, blk), F32),
            pltpu.VMEM((2, levels * rows, blk), F32),
            pltpu.VMEM((2, levels, 1, 2 * levels), F32),
            pltpu.VMEM((2, STEPS, 1, levels), F32),
            pltpu.VMEM((2, 1, levels), F32),
            pltpu.VMEM((2, HALF, REACH, blk), F32),
            pltpu.VMEM((HALF, REACH, blk), F32),
            pltpu.VMEM((nz, HALF, GROUP, blk), F32),
            pltpu.VMEM((2, GROUP, blk), F32),
            pltpu.VMEM((2, blk), F32),
            pltpu.VMEM((nz, 2, blk), F32),
            pltpu.VMEM((nz * GROUP, blk), F32),
            pltpu.VMEM((nw, HALF, 2, blk), F32),
            pltpu.VMEM((nw, HALF, 2, blk), F32),
            pltpu.VMEM((2, HALF, 2, blk), F32),
            pltpu.VMEM((nw, REACH, blk), F32),
            pltpu.VMEM((nw, REACH, blk), F32),
            pltpu.VMEM((2, REACH, blk), F32),
            pltpu.VMEM((REACH, blk), F32),
            dma((8,)),
            dma((4,)),
            dma((4,)),
        ]
        + [dma] * 14,
        compiler_params=pltpu.CompilerParams(
            has_side_effects=True, collective_id=0, vmem_limit_bytes=32 << 20
        ),
    )(
        *(pltpu.with_memory_space_constraint(array, pltpu.HBM) for array in arrays)
    )
    return out.reshape(1, levels, cells)


def solution(mesh):
    return jax.shard_map(
        on_device,
        mesh=mesh,
        in_specs=(
            P("comp", "lev", "tile"),
            P("comp", "lev", None),
            P("comp", None, "lev"),
            P("comp", "lev"),
            P(),
            P("tile", None),
            P("tile"),
            P("tile", None, None, None),
        ),
        out_specs=P("comp", "lev", "tile"),
        check_vma=False,
    )
```
